256 devices in a mesh: section: 8 (over z), expert: 32 (over x, y, core).
Axes of the slice: x: 4, y: 4, z: 8, core: 2. Of those that a mesh axis runs over, the one named last changes fastest.
Arguments:
- emitted: bfloat16 [8, 2, 2048, 2048], P('section', None, 'expert'), may hold values from -6 to 6
- levels: int32 [8, 2, 2048], P('section', None, 'expert'), may hold values from 0 to 999
- expert_ids: int32 [8, 2, 2048, 6], P('section', None, 'expert'), may hold values from 0 to 31, all different within a row; in each aligned block of 64 rows (0 to 63, 64 to 127, ..., all dimensions but the last counted through in order) at most 16 rows name the same one
- gate_values: float32 [8, 2, 2048, 6], P('section', None, 'expert'), may hold values from 0.05 to 0.5
- w_gate: bfloat16 [8, 32, 2048, 768], P('section', 'expert'), may hold values from -0.125 to 0.125
- w_up: bfloat16 [8, 32, 2048, 768], P('section', 'expert'), may hold values from -0.125 to 0.125
- w_down: bfloat16 [8, 32, 768, 2048], P('section', 'expert'), may hold values from -0.21875 to 0.21875
- w_mod: bfloat16 [8, 256, 4096], P('section'), may hold values from -0.375 to 0.375
Outputs:
- layer_out: bfloat16 [8, 2, 2048, 2048], P('section', None, 'expert')
The draws below stay inside these ranges and needn't reach their ends.
Inputs may be any that keep to these rules, and one draw needn't show every extreme that they name: `expert_ids`: each token names 6 different experts. Among the 64 tokens of one device of expert in one microbatch at one section, no expert is named by more than 16 tokens, and in every draw some expert is named by exactly 16 of them.
All inputs are finite; a program needn't handle non-finite values.
Results may differ from the reference program's by a relative error of at most 0.006.
Values may be sent and summed in bfloat16 or wider, within the bound.
A program may use at most 64 MiB of HBM per device.

```python
import math
import jax
import jax.numpy as jnp
import numpy as np
from jax import lax

D = 2048
FF = 768
TOP = 6
FREQ = 256
LEVELS = 1000
MB = 2
TOK_DEV = 64
SECTIONS = 8
EXPERTS = 32
CAP = 16
TOKENS = 2048
N_SECTION = 8
N_EXPERT = 32


def touch_ends(values, rng, smallest, top_value):
    longest = values.shape.index(max(values.shape))
    spots = []
    for shift in (0, 1):
        where = [jax.random.randint(jax.random.fold_in(rng, axis), (), 0, length) for axis, length in enumerate(values.shape)]
        where[longest] = (where[longest] + shift) % values.shape[longest]
        spots.append(tuple(where))
    return values.at[spots[0]].set(smallest).at[spots[1]].set(top_value)


def block_levels(own_key, extent, shards, low, top_value):
    factor_of = 1.0
    for dim, blocks in shards:
        draws = jax.random.uniform(jax.random.fold_in(jax.random.fold_in(own_key, 6), dim), (blocks,), jnp.float32, low / len(shards), top_value / len(shards))
        factor_of = factor_of * jnp.repeat(jnp.exp(draws), extent[dim] // blocks).reshape((-1,) + (1,) * (len(extent) - 1 - dim))
    return factor_of


def assign_block(rng, own, number, rows, number_of, top, most, slope):
    order = jax.random.permutation(rng, number_of)
    crowded, common = portions_of(number_of, rows * top, most, slope, True), portions_of(number_of, rows * top, most, slope, False)
    places = jnp.arange(number_of)

    def named(sizes, turn):
        used = int((sizes > 0).sum())
        fixed = max(1, used // 4)
        moved = fixed + (places - fixed + turn * (used - fixed)) % max(1, number_of - fixed)
        return jnp.zeros((number_of,), jnp.int32).at[order[jnp.where(places < fixed, places, moved)]].set(jnp.asarray(sizes, jnp.int32))

    sizes = jnp.where(number % 4 == 0, named(crowded, number // 4), named(common, number - number // 4 - 1))
    mixed = jax.random.permutation(jax.random.fold_in(own, 3), number_of)
    source_of, taker = mixed[0:number_of // 2 * 2:2], mixed[1:number_of // 2 * 2:2]
    room = jnp.minimum(sizes[source_of] - 1, most - sizes[taker]) // 2
    room = jnp.where((source_of == order[0]) | (taker == order[0]) | (sizes[taker] == 0), 0, jnp.maximum(room, 0))
    moved = jax.random.randint(jax.random.fold_in(own, 4), (number_of // 2,), 0, 1 << 20) % (room + 1)
    sizes = sizes.at[source_of].add(-moved).at[taker].add(moved)
    items = jnp.searchsorted(jnp.cumsum(sizes), jnp.arange(rows * top), side="right").astype(jnp.int32)
    grid = items.reshape(top, rows).T
    grid = grid[jax.random.permutation(jax.random.fold_in(own, 1), rows)]
    turn = jax.random.randint(jax.random.fold_in(own, 2), (rows, 1), 0, top)
    return jnp.take_along_axis(grid, (jnp.arange(top)[None, :] + turn) % top, axis=1)


def portions_of(amount, total, reach, lean, full):
    loads = [(1 << 20) // math.isqrt(standing ** lean) + 1 for standing in range(1, amount + 1)]
    largest = reach if full else min(reach, max(-(-total // amount), total * loads[0] // sum(loads)))
    least = 1 if total - largest >= amount - 1 else 0
    holding, spare = [largest] + [least] * (amount - 1), total - largest - least * (amount - 1)
    while spare > 0:
        free = [i for i in range(1, amount) if holding[i] < largest] or [i for i in range(1, amount) if holding[i] < reach]
        mass, remaining = sum([loads[i] for i in free]), spare
        for i in free:
            extra = min(reach - holding[i], max(1, remaining * loads[i] // mass), spare)
            holding[i] = holding[i] + extra
            spare = spare - extra
    return np.array(holding)


def noise(own_key, extent, deviation, most, pieces=(), held_as=jnp.bfloat16):
    drawn = deviation * jax.random.normal(own_key, extent, jnp.float32)
    if pieces:
        drawn = drawn * block_levels(own_key, extent, pieces, -0.22, 0.18)
    return jnp.clip(drawn, -most, most).astype(held_as)


def setup_inputs(seed: int = 0) -> dict:
    keys = jax.random.split(jax.random.key(seed), 9)
    emitted = noise(keys[0], (SECTIONS, MB, TOKENS, D), 1.0, 6.0, ((0, 8), (2, 32)))
    levels = touch_ends(jax.random.randint(keys[1], (SECTIONS, MB, TOKENS), 0, LEVELS), jax.random.fold_in(keys[1], 1), 0, LEVELS - 1).astype(jnp.int32)
    expert_ids_keys = jax.random.split(jax.random.fold_in(keys[2], 1), SECTIONS * MB * TOKENS // TOK_DEV)
    expert_ids_turns = jax.random.permutation(jax.random.fold_in(keys[2], 3), SECTIONS * MB * TOKENS // TOK_DEV)
    expert_ids = jax.vmap(lambda own, number: assign_block(jax.random.fold_in(keys[2], 2), own, number, TOK_DEV, EXPERTS, TOP, CAP, 2))(expert_ids_keys, expert_ids_turns).reshape((SECTIONS, MB, TOKENS, TOP))
    gate_values = jnp.clip(0.05 + 0.45 * jax.random.uniform(keys[3], (SECTIONS, MB, TOKENS, TOP), jnp.float32) ** block_levels(keys[3], (SECTIONS, MB, TOKENS, TOP), ((0, 8), (2, 32)), -0.2, 0.2), 0.05, 0.5)
    w_gate = noise(keys[4], (SECTIONS, EXPERTS, D, FF), D ** -0.5, 0.125, ((0, 8), (1, 32)))
    w_up = noise(keys[5], (SECTIONS, EXPERTS, D, FF), D ** -0.5, 0.125, ((0, 8), (1, 32)))
    w_down = noise(keys[6], (SECTIONS, EXPERTS, FF, D), FF ** -0.5, 0.21875, ((0, 8), (1, 32)))
    w_mod = noise(keys[7], (SECTIONS, FREQ, 2 * D), FREQ ** -0.5, 0.375, ((0, 8),))
    return dict(emitted=emitted, levels=levels, expert_ids=expert_ids, gate_values=gate_values, w_gate=w_gate, w_up=w_up, w_down=w_down, w_mod=w_mod)


epsilon = 1e-06

def level_embedding(levels, entries):
    half_width = entries // 2
    frequency = jnp.exp(-math.log(10000.0) * jnp.arange(half_width, dtype=jnp.float32) / half_width)
    angles = levels.astype(jnp.float32)[:, None] * frequency[None, :]
    return jnp.concatenate([jnp.cos(angles), jnp.sin(angles)], axis=1).astype(jnp.bfloat16)

def modulate(tokens_in, levels, mod_weight):
    features = tokens_in.shape[1]
    embed = level_embedding(levels, mod_weight.shape[0])
    modulation = jnp.dot(embed, mod_weight, preferred_element_type=jnp.float32)
    values = tokens_in.astype(jnp.float32)
    mean_square = lax.optimization_barrier(jnp.mean(values * values, axis=1, keepdims=True))
    normed = values * lax.rsqrt(mean_square + epsilon) * (1.0 + modulation[:, :features]) + modulation[:, features:]
    return normed.astype(jnp.bfloat16)

def slot_table(id_block, experts):
    flat_ids = id_block.reshape(-1).astype(jnp.int32)
    onehot = (flat_ids[:, None] == jnp.arange(experts, dtype=jnp.int32)[None, :]).astype(jnp.int32)
    before = jnp.cumsum(onehot, axis=0) - onehot
    slot_pos = lax.optimization_barrier(jnp.sum(before * onehot, axis=1)).astype(jnp.int32)
    return (flat_ids, slot_pos)

def fill_buffer(normed, flat_ids, slot_pos, experts, capacity):
    chosen = flat_ids.shape[0] // normed.shape[0]
    token_index = (jnp.arange(flat_ids.shape[0], dtype=jnp.int32) // chosen).astype(jnp.int32)
    placing = (flat_ids * capacity + slot_pos).astype(jnp.int32)
    buffer = jnp.zeros((experts * capacity, normed.shape[1]), normed.dtype)
    buffer = buffer.at[placing].set(normed[token_index])
    return (buffer.reshape(experts, capacity, normed.shape[1]), placing)

def expert_rows(received, gate_weight, up_weight, down_weight):
    sources, per_source, features = received.shape
    row_data = received.reshape(sources * per_source, features)
    gate_part = jnp.dot(row_data, gate_weight, preferred_element_type=jnp.float32)
    up_part = jnp.dot(row_data, up_weight, preferred_element_type=jnp.float32)
    hidden = (jax.nn.silu(gate_part) * up_part).astype(jnp.bfloat16)
    produced = jnp.dot(hidden, down_weight, preferred_element_type=jnp.float32).astype(jnp.bfloat16)
    return produced.reshape(sources, per_source, features)

def combine(tokens_in, returned, placing, gate_block):
    count_rows, chosen = gate_block.shape
    features = tokens_in.shape[1]
    picked = returned.reshape(-1, features)[placing].astype(jnp.float32).reshape(count_rows, chosen, features)
    combined = tokens_in.astype(jnp.float32) + lax.optimization_barrier(jnp.sum(gate_block[:, :, None].astype(jnp.float32) * picked, axis=1))
    return combined.astype(jnp.bfloat16)

def run_expert(packed):
    return expert_rows(packed[0], packed[1], packed[2], packed[3])

def reference(emitted, levels, expert_ids, gate_values, w_gate, w_up, w_down, w_mod):
    arrived = jnp.roll(emitted, 1, axis=0)

    def build_block(normed_block, id_block):
        flat_ids, slot_pos = slot_table(id_block, EXPERTS)
        return fill_buffer(normed_block, flat_ids, slot_pos, EXPERTS, CAP)
    section_outs = []
    for section_index in range(N_SECTION):
        batch_outs = []
        for batch_index in range(MB):
            tokens_in = arrived[section_index, batch_index]
            normed = modulate(tokens_in, levels[section_index, batch_index], w_mod[section_index])
            normed_blocks = normed.reshape(N_EXPERT, TOK_DEV, D)
            id_blocks = expert_ids[section_index, batch_index].reshape(N_EXPERT, TOK_DEV, TOP)
            buffers, placings = jax.vmap(build_block)(normed_blocks, id_blocks)
            by_expert = jnp.swapaxes(buffers, 0, 1)
            produced = lax.map(run_expert, (by_expert, w_gate[section_index], w_up[section_index], w_down[section_index]))
            returned = jnp.swapaxes(produced, 0, 1)
            gate_blocks = gate_values[section_index, batch_index].reshape(N_EXPERT, TOK_DEV, TOP)
            token_blocks = tokens_in.reshape(N_EXPERT, TOK_DEV, D)
            outs = jax.vmap(combine)(token_blocks, returned, placings, gate_blocks)
            batch_outs.append(outs.reshape(TOKENS, D))
        section_outs.append(jnp.stack(batch_outs))
    return jnp.stack(section_outs)
```

```python
import math

import jax
import jax.numpy as jnp
from jax import lax
from jax.sharding import PartitionSpec as P

epsilon = 1e-06


def shifted(value, axis, steps):
    count = lax.axis_size(axis)
    pairs = [(source, (source + steps) % count) for source in range(count)]
    return lax.ppermute(value, axis, pairs)


def level_embedding(levels, entries):
    half_width = entries // 2
    frequency = jnp.exp(-math.log(10000.0) * jnp.arange(half_width, dtype=jnp.float32) / half_width)
    angles = levels.astype(jnp.float32)[:, None] * frequency[None, :]
    return jnp.concatenate([jnp.cos(angles), jnp.sin(angles)], axis=1).astype(jnp.bfloat16)


def modulate(tokens_in, levels, mod_weight):
    features = tokens_in.shape[1]
    embed = level_embedding(levels, mod_weight.shape[0])
    modulation = jnp.dot(embed, mod_weight, preferred_element_type=jnp.float32)
    values = tokens_in.astype(jnp.float32)
    mean_square = jnp.mean(values * values, axis=1, keepdims=True)
    normed = (
        values * lax.rsqrt(mean_square + epsilon) * (1.0 + modulation[:, :features])
        + modulation[:, features:]
    )
    return normed.astype(jnp.bfloat16)


def slot_map(id_block, experts):
    rows = id_block.shape[0]
    named = jnp.sum(
        (id_block[:, :, None] == jnp.arange(experts, dtype=jnp.int32)[None, None, :]), axis=1
    ).astype(jnp.bfloat16)
    order = jnp.arange(rows, dtype=jnp.int32)
    earlier = (order[:, None] > order[None, :]).astype(jnp.bfloat16)
    before = jnp.dot(earlier, named, preferred_element_type=jnp.float32)
    return jnp.where(named > 0, before, -1.0)


def fill_buffer(normed, slots, capacity):
    rows, experts = slots.shape
    places = jnp.arange(capacity, dtype=jnp.float32)
    select = (slots.T[:, None, :] == places[None, :, None]).astype(jnp.bfloat16)
    buffer = jnp.dot(
        select.reshape(experts * capacity, rows), normed, preferred_element_type=jnp.float32
    ).astype(jnp.bfloat16)
    return buffer.reshape(experts, capacity, normed.shape[1])


def expert_rows(received, gate_weight, up_weight, down_weight):
    sources, per_source, features = received.shape
    row_data = received.reshape(sources * per_source, features)
    gate_part = jnp.dot(row_data, gate_weight, preferred_element_type=jnp.float32)
    up_part = jnp.dot(row_data, up_weight, preferred_element_type=jnp.float32)
    hidden = (jax.nn.silu(gate_part) * up_part).astype(jnp.bfloat16)
    produced = jnp.dot(hidden, down_weight, preferred_element_type=jnp.float32).astype(jnp.bfloat16)
    return produced.reshape(sources, per_source, features)


def combine(tokens_in, returned, slots, id_block, gate_block):
    rows, experts = slots.shape
    capacity, features = returned.shape[1], returned.shape[2]
    gate_map = jnp.sum(
        jnp.where(
            id_block[:, :, None] == jnp.arange(experts, dtype=jnp.int32)[None, None, :],
            gate_block[:, :, None],
            0.0,
        ),
        axis=1,
    )
    places = jnp.arange(capacity, dtype=jnp.float32)
    weights = jnp.where(slots[:, :, None] == places[None, None, :], gate_map[:, :, None], 0.0)
    weights = weights.reshape(rows, experts * capacity)
    high = weights.astype(jnp.bfloat16)
    low = (weights - high.astype(jnp.float32)).astype(jnp.bfloat16)
    both = jnp.dot(
        jnp.concatenate([high, low], axis=0),
        returned.reshape(experts * capacity, features),
        preferred_element_type=jnp.float32,
    )
    return (tokens_in.astype(jnp.float32) + both[:rows] + both[rows:]).astype(jnp.bfloat16)


def shards(emitted, levels, expert_ids, gate_values, w_gate, w_up, w_down, w_mod):
    arrived = shifted(emitted, "section", 1)
    experts = lax.axis_size("expert")
    batches = emitted.shape[1]
    tok_rows = emitted.shape[2]
    chosen = expert_ids.shape[3]
    capacity = min(tok_rows, 4 * tok_rows * chosen // (3 * experts))
    gate_weight = w_gate[0, 0]
    up_weight = w_up[0, 0]
    down_weight = w_down[0, 0]
    prepared = []
    for batch_index in range(batches):
        normed = modulate(arrived[0, batch_index], levels[0, batch_index], w_mod[0])
        slots = slot_map(expert_ids[0, batch_index], experts)
        prepared.append((fill_buffer(normed, slots, capacity), slots))
    results = []
    for batch_index in range(batches):
        produced = expert_rows(
            lax.all_to_all(
                prepared[batch_index][0], "expert", split_axis=0, concat_axis=0, tiled=True
            ),
            gate_weight,
            up_weight,
            down_weight,
        )
        returned = lax.all_to_all(produced, "expert", split_axis=0, concat_axis=0, tiled=True)
        results.append(
            combine(
                arrived[0, batch_index],
                returned,
                prepared[batch_index][1],
                expert_ids[0, batch_index],
                gate_values[0, batch_index],
            )
        )
    return jnp.stack(results)[None]


def solution(mesh):
    placed = (
        P("section", None, "expert", None),
        P("section", None, "expert"),
        P("section", None, "expert", None),
        P("section", None, "expert", None),
        P("section", "expert", None, None),
        P("section", "expert", None, None),
        P("section", "expert", None, None),
        P("section", None, None),
    )
    return jax.shard_map(
        shards,
        mesh=mesh,
        in_specs=placed,
        out_specs=P("section", None, "expert", None),
        check_vma=False,
    )
```

```python
import functools
import math

import jax
import jax.numpy as jnp
from jax import lax
from jax.experimental import pallas as pl
from jax.experimental.pallas import tpu as pltpu
from jax.sharding import PartitionSpec as P

epsilon = 1e-06
MESH = pl.DeviceIdType.MESH
F32, BF16 = jnp.float32, jnp.bfloat16
SIDE = 4
SLOTS = 16
BLOCK = 64
HALF = BLOCK // 2
PICKS = SIDE * 2 * SLOTS


def level_embedding(levels, entries):
    half_width = entries // 2
    frequency = jnp.exp(-math.log(10000.0) * jnp.arange(half_width, dtype=F32) / half_width)
    angles = levels.astype(F32)[:, None] * frequency[None, :]
    return jnp.concatenate([jnp.cos(angles), jnp.sin(angles)], axis=1).astype(BF16)


def layer_kernel(
    sections, top,
    emitted, embed, ids, gates, w_gate, w_up, w_down, w_mod,
    out,
    vg, vu, vd, vm, mod, meta, weigh,
    arrived, gathered, picked, passed, rows_in, rows_out, passed_back, returned,
    parts, half_in, part_in, total,
    load_sem, z_send, z_recv, m_send, m_recv, g_send, g_recv, gf_send,
    b_send, b_recv, f_recv, f_send, o_send, o_recv, p_recv, p_send, h_send, h_recv, q_send, q_recv,
):
    section = lax.axis_index("section")
    place = lax.axis_index("expert")
    x, y, core = place // 8, (place // 2) % SIDE, place % 2
    features = arrived.shape[2]

    def at(dx, dy, other):
        seat = core + other * (1 - 2 * core)
        return (section, ((x + dx + 8) % SIDE) * 8 + ((y + dy + 8) % SIDE) * 2 + seat)

    def along(batch, da, db, other):
        return at(da + batch * (db - da), db + batch * (da - db), other)

    def remote(src, dst, send, recv, device):
        return pltpu.make_async_remote_copy(
            src_ref=src, dst_ref=dst, send_sem=send, recv_sem=recv, device_id=device, device_id_type=MESH
        )

    def got(dst, recv):
        remote(dst, dst, recv, recv, (section, place)).wait_recv()

    def left(src, send):
        remote(src, src, send, send, (section, place)).wait_send()

    after = ((section + 1) % sections, place)
    ahead = ((section + sections - 1) % sections, place)

    loads = [
        pltpu.make_async_copy(w_mod.at[0], vm, load_sem.at[0]),
        pltpu.make_async_copy(w_gate.at[0, 0], vg, load_sem.at[1]),
        pltpu.make_async_copy(w_up.at[0, 0], vu, load_sem.at[2]),
        pltpu.make_async_copy(w_down.at[0, 0], vd, load_sem.at[3]),
    ]
    loads[0].start()

    barrier = pltpu.get_barrier_semaphore()
    friends = [after, ahead, at(0, 0, 1), at(2, 0, 0), at(0, 2, 0)]
    for step in (1, -1):
        for other in (0, 1):
            friends += [at(step, 0, other), at(0, step, other)]
    for friend in friends:
        pl.semaphore_signal(barrier, inc=1, device_id=friend, device_id_type=MESH)
    pl.semaphore_wait(barrier, len(friends))

    def shift(piece):
        batch, rows = piece % 2, pl.ds(pl.multiple_of((piece // 2) * HALF, HALF), HALF)
        return remote(
            emitted.at[0, batch, rows], arrived.at[batch, rows], z_send.at[piece], z_recv.at[piece], after
        )

    for piece in range(4):
        shift(piece).start()
    for load in loads[1:]:
        load.start()

    number = ids[...]
    experts = SIDE * SIDE * 2
    name = lax.broadcasted_iota(jnp.int32, (experts, 2 * BLOCK), 0)
    named = jnp.zeros((experts, 2 * BLOCK), F32)
    for k in range(top):
        named = named + jnp.where(number[k : k + 1, :] == name, 1.0, 0.0)
    row = lax.broadcasted_iota(jnp.int32, (2 * BLOCK, 2 * BLOCK), 0)
    col = lax.broadcasted_iota(jnp.int32, (2 * BLOCK, 2 * BLOCK), 1)
    earlier = jnp.where((row < col) & (row // BLOCK == col // BLOCK), 1.0, 0.0).astype(BF16)
    before = jnp.dot(named.astype(BF16), earlier, preferred_element_type=F32)
    lane = lax.broadcasted_iota(jnp.int32, (1, 2 * BLOCK), 1)
    for batch in range(2):
        meta[batch, 0] = jnp.full((16, 2 * BLOCK), -1.0, F32)
    for k in range(top):
        slot = jnp.sum(jnp.where(number[k : k + 1, :] == name, before, 0.0), axis=0, keepdims=True)
        code = number[k : k + 1, :].astype(F32) * SLOTS + slot
        gate = gates[k : k + 1, :]
        for batch in range(2):
            mine = lane // BLOCK == batch
            shown = jnp.where(mine, code, -1.0)
            worth = jnp.where(mine, gate, 0.0)
            if batch:
                shown = pltpu.roll(shown, BLOCK, 1)
                worth = pltpu.roll(worth, BLOCK, 1)
            meta[batch, 0, k : k + 1, :] = shown
            meta[batch, 0, 8 + k : 9 + k, :] = worth

    def tell(batch, step):
        return remote(
            meta.at[batch, 0], meta.at[batch, step], m_send.at[batch, step - 1], m_recv.at[batch, step - 1],
            along(batch, step, 0, 0),
        )

    for batch in range(2):
        for step in (1, 2, 3):
            tell(batch, step).start()

    loads[0].wait()
    mod[...] = jnp.dot(embed[...], vm[...], preferred_element_type=F32)

    def spread(batch, part, way):
        rows = pl.ds(pl.multiple_of(part * HALF, HALF), HALF)
        return remote(
            gathered.at[batch, 0, rows], gathered.at[batch, 1 + 2 * way, rows],
            g_send.at[batch, way, part], g_recv.at[batch, 2 * way, part],
            along(batch, 1 - 2 * way, 0, 0),
        )

    def normalize(piece, carry):
        batch, part = piece % 2, piece // 2
        rows = pl.ds(pl.multiple_of(part * HALF, HALF), HALF)
        got(arrived.at[batch, rows], z_recv.at[piece])
        values = arrived[batch, rows, :].astype(F32)
        mean_square = jnp.mean(values * values, axis=1, keepdims=True)
        own = pl.ds(pl.multiple_of(batch * BLOCK + part * HALF, HALF), HALF)
        normed = values * lax.rsqrt(mean_square + epsilon) * (1.0 + mod[own, :features]) + mod[own, features:]
        gathered[batch, 0, rows, :] = normed.astype(BF16)
        spread(batch, part, 0).start()
        spread(batch, part, 1).start()
        return carry

    lax.fori_loop(0, 4, normalize, 0)

    def hand_on(batch, way):
        rows = pl.ds(way * HALF, HALF)
        return remote(
            gathered.at[batch, 1 + 2 * way, rows], gathered.at[batch, 2, rows],
            gf_send.at[batch, way], g_recv.at[batch, 1, way],
            along(batch, 1 - 2 * way, 0, 0),
        )

    pick = lax.broadcasted_iota(jnp.int32, (PICKS, 2 * BLOCK), 0)
    far, other, slot = pick // (2 * SLOTS), (pick // SLOTS) % 2, pick % SLOTS
    seat = core + other * (1 - 2 * core)

    def select(batch, step):
        line = jnp.where(
            batch == 0,
            x * 8 + ((y + far) % SIDE) * 2,
            ((x + far) % SIDE) * 8 + y * 2,
        )
        wanted = ((line + seat) * SLOTS + slot).astype(F32)
        hit = jnp.zeros((PICKS, 2 * BLOCK), F32)
        worth = jnp.zeros((PICKS, 2 * BLOCK), F32)
        for k in range(top):
            same = meta[batch, step, k : k + 1, :] == wanted
            hit = jnp.where(same, 1.0, hit)
            worth = jnp.where(same, meta[batch, step, 8 + k : 9 + k, :], worth)
        worth = worth.T
        high = worth[:BLOCK].astype(BF16)
        weigh[batch, step, :BLOCK, :] = high
        weigh[batch, step, BLOCK:, :] = (worth[:BLOCK] - high.astype(F32)).astype(BF16)
        chosen = jnp.dot(hit[:, :BLOCK].astype(BF16), gathered[batch, step], preferred_element_type=F32)
        picked[batch, :, :, step] = chosen.astype(BF16).reshape(SIDE, 2, SLOTS, features)

    def select_own(batch, carry):
        select(batch, 0)
        return carry

    lax.fori_loop(0, 2, select_own, 0)

    for batch in range(2):
        for way in range(2):
            rows = pl.ds(way * HALF, HALF)
            got(gathered.at[batch, 1 + 2 * way, rows], g_recv.at[batch, 2 * way, way])
            hand_on(batch, way).start()
            rows = pl.ds((1 - way) * HALF, HALF)
            got(gathered.at[batch, 1 + 2 * way, rows], g_recv.at[batch, 2 * way, 1 - way])
            got(meta.at[batch, 1 + 2 * way], m_recv.at[batch, 2 * way])

    def select_near(piece, carry):
        select(piece % 2, 1 + 2 * (piece // 2))
        return carry

    lax.fori_loop(0, 4, select_near, 0)

    def exchange(batch, step, other):
        if step == 2:
            return remote(
                picked.at[batch, 2, other], passed.at[batch, other], b_send.at[batch, 2, other], f_recv.at[batch, other],
                along(batch, 0, 1 - 2 * other, 0),
            )
        return remote(
            picked.at[batch, step, other], rows_in.at[batch, step, other], b_send.at[batch, step, other],
            b_recv.at[batch, step, other], along(batch, 0, step, other),
        )

    def pass_on(batch, other):
        return remote(
            passed.at[batch, other], rows_in.at[batch, 2, other], f_send.at[batch, other], b_recv.at[batch, 2, other],
            along(batch, 0, 1 - 2 * other, other),
        )

    order = [(2, 0), (2, 1), (1, 0), (3, 0), (1, 1), (3, 1), (0, 1)]

    def select_far(batch, carry):
        for way in range(2):
            got(gathered.at[batch, 2, pl.ds(way * HALF, HALF)], g_recv.at[batch, 1, way])
        got(meta.at[batch, 2], m_recv.at[batch, 1])
        select(batch, 2)
        for step, other in order:
            exchange(batch, step, other).start()
        pltpu.make_async_copy(picked.at[batch, 0, 0], rows_in.at[batch, 0, 0], b_recv.at[batch, 0, 0]).start()
        return carry

    lax.fori_loop(0, 2, select_far, 0)

    for load in loads[1:]:
        load.wait()

    def back(batch, step, other):
        return remote(
            rows_out.at[batch, step, other], returned.at[batch, step, other], o_send.at[batch, step, other],
            o_recv.at[batch, step, other], along(batch, 0, 4 - step, other),
        )

    def back_far(batch, other):
        return remote(
            rows_out.at[batch, 2, other], passed_back.at[batch, other], o_send.at[batch, 2, other],
            p_recv.at[batch, other], along(batch, 0, 2 * other - 1, 0),
        )

    def pass_back(batch, other):
        return remote(
            passed_back.at[batch, other], returned.at[batch, 2, other], p_send.at[batch, other],
            o_recv.at[batch, 2, other], along(batch, 0, 2 * other - 1, other),
        )

    def work(piece, carry):
        batch, turn = piece % 2, piece // 2
        step = turn + turn // 2 - 2 * (turn // 3)

        @pl.when(piece == 2)
        def _():
            for one in range(2):
                for other in range(2):
                    got(passed.at[one, other], f_recv.at[one, other])
                    pass_on(one, other).start()

        got(rows_in.at[batch, step, 0], b_recv.at[batch, step, 0])
        got(rows_in.at[batch, step, 1], b_recv.at[batch, step, 1])
        rows = rows_in[batch, step].reshape(2 * SIDE * SLOTS, features)
        gate_part = jnp.dot(rows, vg[...], preferred_element_type=F32)
        up_part = jnp.dot(rows, vu[...], preferred_element_type=F32)
        hidden = (gate_part / (1.0 + jnp.exp(-gate_part)) * up_part).astype(BF16)
        produced = jnp.dot(hidden, vd[...], preferred_element_type=F32).astype(BF16)
        rows_out[batch, step] = produced.reshape(2, SIDE, SLOTS, features)

        @pl.when(step == 0)
        def _():
            pltpu.make_async_copy(rows_out.at[batch, 0, 0], returned.at[batch, 0, 0], o_recv.at[batch, 0, 0]).start()
            back(batch, 0, 1).start()

        @pl.when(step % 2 == 1)
        def _():
            back(batch, step, 0).start()
            back(batch, step, 1).start()

        @pl.when(step == 2)
        def _():
            back_far(batch, 0).start()
            back_far(batch, 1).start()

        return carry

    lax.fori_loop(0, 8, work, 0)

    for batch in range(2):
        for other in range(2):
            got(passed_back.at[batch, other], p_recv.at[batch, other])
            pass_back(batch, other).start()

    def add_up(batch, step):
        rows = returned[batch, :, :, step].reshape(PICKS, features)
        both = jnp.dot(weigh[batch, step], rows, preferred_element_type=F32)
        return both[:BLOCK] + both[BLOCK:]

    def sum_half(batch, way):
        rows = pl.ds(way * HALF, HALF)
        return remote(
            parts.at[batch, 1, rows], half_in.at[batch, way], h_send.at[batch, way], h_recv.at[batch, way],
            along(batch, 2 * way - 1, 0, 0),
        )

    def sum_home(batch, way):
        return remote(
            parts.at[batch, 2 * way], part_in.at[batch, way], q_send.at[batch, way], q_recv.at[batch, way],
            along(batch, 2 * way - 1, 0, 0),
        )

    def add_far(batch, carry):
        for step in range(SIDE):
            for other in range(2):
                got(returned.at[batch, step, other], o_recv.at[batch, step, other])
        parts[batch, 1] = add_up(batch, 2).astype(BF16)
        sum_half(batch, 0).start()
        sum_half(batch, 1).start()
        return carry

    lax.fori_loop(0, 2, add_far, 0)

    def add_near(batch, carry):
        total[batch] = add_up(batch, 0) + arrived[batch].astype(F32)
        for way in range(2):
            near = add_up(batch, 1 + 2 * way)
            got(half_in.at[batch, way], h_recv.at[batch, way])
            held = half_in[batch, way].astype(F32)
            if way == 0:
                parts[batch, 0, :HALF] = (near[:HALF] + held).astype(BF16)
                parts[batch, 0, HALF:] = near[HALF:].astype(BF16)
            else:
                parts[batch, 2, :HALF] = near[:HALF].astype(BF16)
                parts[batch, 2, HALF:] = (near[HALF:] + held).astype(BF16)
            sum_home(batch, way).start()
        return carry

    lax.fori_loop(0, 2, add_near, 0)

    def finish(batch, carry):
        got(part_in.at[batch, 0], q_recv.at[batch, 0])
        got(part_in.at[batch, 1], q_recv.at[batch, 1])
        final = total[batch] + part_in[batch, 0].astype(F32) + part_in[batch, 1].astype(F32)
        out[batch] = final.astype(BF16)
        return carry

    lax.fori_loop(0, 2, finish, 0)

    for piece in range(4):
        shift(piece).wait_send()
    for batch in range(2):
        for step in (1, 2, 3):
            tell(batch, step).wait_send()
        for way in range(2):
            spread(batch, 0, way).wait_send()
            spread(batch, 1, way).wait_send()
            hand_on(batch, way).wait_send()
            pass_on(batch, way).wait_send()
            pass_back(batch, way).wait_send()
            sum_half(batch, way).wait_send()
            sum_home(batch, way).wait_send()
            back_far(batch, way).wait_send()
        for step, other in order:
            exchange(batch, step, other).wait_send()
        for step, other in ((1, 0), (1, 1), (3, 0), (3, 1), (0, 1)):
            back(batch, step, other).wait_send()


def shards(emitted, levels, expert_ids, gate_values, w_gate, w_up, w_down, w_mod):
    batches, rows, features = emitted.shape[1:]
    top, inner = expert_ids.shape[3], w_gate.shape[3]
    tokens = batches * rows
    embed = level_embedding(levels.reshape(tokens), w_mod.shape[1])
    ids = expert_ids.reshape(tokens, top).T
    gates = gate_values.reshape(tokens, top).T
    anywhere, vmem = pl.BlockSpec(memory_space=pl.ANY), pl.BlockSpec(memory_space=pltpu.VMEM)
    dma = pltpu.SemaphoreType.DMA
    out = pl.pallas_call(
        functools.partial(layer_kernel, lax.axis_size("section"), top),
        out_shape=jax.ShapeDtypeStruct((batches, rows, features), BF16),
        in_specs=[anywhere, vmem, vmem, vmem, anywhere, anywhere, anywhere, anywhere],
        out_specs=vmem,
        scratch_shapes=[
            pltpu.VMEM((features, inner), BF16),
            pltpu.VMEM((features, inner), BF16),
            pltpu.VMEM((inner, features), BF16),
            pltpu.VMEM(w_mod.shape[1:], BF16),
            pltpu.VMEM((tokens, 2 * features), F32),
            pltpu.VMEM((2, SIDE, 16, 2 * BLOCK), F32),
            pltpu.VMEM((2, SIDE, 2 * BLOCK, PICKS), BF16),
            pltpu.VMEM((2, BLOCK, features), BF16),
            pltpu.VMEM((2, SIDE, BLOCK, features), BF16),
            pltpu.VMEM((2, SIDE, 2, SIDE, SLOTS, features), BF16),
            pltpu.VMEM((2, 2, SIDE, SLOTS, features), BF16),
            pltpu.VMEM((2, SIDE, 2, SIDE, SLOTS, features), BF16),
            pltpu.VMEM((2, SIDE, 2, SIDE, SLOTS, features), BF16),
            pltpu.VMEM((2, 2, SIDE, SLOTS, features), BF16),
            pltpu.VMEM((2, SIDE, 2, SIDE, SLOTS, features), BF16),
            pltpu.VMEM((2, 3, BLOCK, features), BF16),
            pltpu.VMEM((2, 2, HALF, features), BF16),
            pltpu.VMEM((2, 2, BLOCK, features), BF16),
            pltpu.VMEM((2, BLOCK, features), F32),
            dma((4,)), dma((4,)), dma((4,)),
            dma((2, 3)), dma((2, 3)),
            dma((2, 2, 2)), dma((2, 3, 2)), dma((2, 2)),
            dma((2, SIDE, 2)), dma((2, SIDE, 2)), dma((2, 2)), dma((2, 2)),
            dma((2, SIDE, 2)), dma((2, SIDE, 2)), dma((2, 2)), dma((2, 2)),
            dma((2, 2)), dma((2, 2)), dma((2, 2)), dma((2, 2)),
        ],
        compiler_params=pltpu.CompilerParams(
            collective_id=0, has_side_effects=True, vmem_limit_bytes=60 * 1024 * 1024
        ),
    )(emitted, embed, ids, gates, w_gate, w_up, w_down, w_mod)
    return out[None]


def solution(mesh):
    placed = (
        P("section", None, "expert", None),
        P("section", None, "expert"),
        P("section", None, "expert", None),
        P("section", None, "expert", None),
        P("section", "expert", None, None),
        P("section", "expert", None, None),
        P("section", "expert", None, None),
        P("section", None, None),
    )
    return jax.shard_map(
        shards,
        mesh=mesh,
        in_specs=placed,
        out_specs=P("section", None, "expert", None),
        check_vma=False,
    )
```

```python
import functools
import math

import jax
import jax.numpy as jnp
from jax import lax
from jax.experimental import pallas as pl
from jax.experimental.pallas import tpu as pltpu
from jax.sharding import PartitionSpec as P

epsilon = 1e-06
MESH = pl.DeviceIdType.MESH
F32, BF16 = jnp.float32, jnp.bfloat16
SIDE = 4
SLOTS = 16
BLOCK = 64
HALF = BLOCK // 2
PIECE = BLOCK // 4
OFFSET = (0, 1, 3, 2)
PICKS = SIDE * 2 * SLOTS


def layer_kernel(
    sections, top,
    emitted, levels, ids, gates, w_gate, w_up, w_down, w_mod,
    out,
    vg, vu, vd, vm, vl, vi, vw, mod, meta, weigh,
    arrived, gathered, picked, passed, rows_in, rows_out, passed_back, returned,
    far_part, near_part, near_held, half_in, part_in, total,
    load_sem, z_send, z_recv, m_send, m_recv, g_send, g_recv, gf_send, gf_recv,
    b_send, b_recv, f_recv, f_send, o_send, o_recv, p_recv, p_send, h_send, h_recv, q_send, q_recv,
):
    section = lax.axis_index("section")
    place = lax.axis_index("expert")
    x, y, core = place // 8, (place // 2) % SIDE, place % 2
    features = arrived.shape[2]

    def at(dx, dy, other):
        seat = core + other * (1 - 2 * core)
        return (section, ((x + dx + 8) % SIDE) * 8 + ((y + dy + 8) % SIDE) * 2 + seat)

    def along(batch, da, db, other):
        return at(da + batch * (db - da), db + batch * (da - db), other)

    def remote(src, dst, send, recv, device):
        return pltpu.make_async_remote_copy(
            src_ref=src, dst_ref=dst, send_sem=send, recv_sem=recv, device_id=device, device_id_type=MESH
        )

    def got(dst, recv):
        remote(dst, dst, recv, recv, (section, place)).wait_recv()

    def left(src, send):
        remote(src, src, send, send, (section, place)).wait_send()

    after = ((section + 1) % sections, place)
    ahead = ((section + sections - 1) % sections, place)

    barrier = pltpu.get_barrier_semaphore()
    friends = [after, ahead, at(0, 0, 1), at(2, 0, 0), at(0, 2, 0)]
    for step in (1, -1):
        for other in (0, 1):
            friends += [at(step, 0, other), at(0, step, other)]
    for friend in friends:
        pl.semaphore_signal(barrier, inc=1, device_id=friend, device_id_type=MESH)

    sources = (levels.at[0], ids.at[0], gates.at[0], w_mod.at[0], w_gate.at[0, 0], w_up.at[0, 0], w_down.at[0, 0])
    targets = (vl, vi, vw, vm, vg, vu, vd)
    loads = [pltpu.make_async_copy(a, b, load_sem.at[i]) for i, (a, b) in enumerate(zip(sources, targets))]
    for load in loads[:4]:
        load.start()
    pl.semaphore_wait(barrier, len(friends))

    def shift(piece):
        batch, rows = piece % 2, pl.ds((piece // 2) * PIECE, PIECE)
        return remote(
            emitted.at[0, batch, rows], arrived.at[batch, rows], z_send.at[piece], z_recv.at[piece], after
        )

    for piece in range(8):
        shift(piece).start()
    for load in loads[4:]:
        load.start()

    for load in loads[:3]:
        load.wait()

    experts = SIDE * SIDE * 2
    name = lax.broadcasted_iota(jnp.int32, (experts, BLOCK), 0)
    row = lax.broadcasted_iota(jnp.int32, (BLOCK, BLOCK), 0)
    col = lax.broadcasted_iota(jnp.int32, (BLOCK, BLOCK), 1)
    earlier = jnp.where(row < col, 1.0, 0.0).astype(BF16)
    for batch in range(2):
        meta[batch, 0] = jnp.full((16, 2 * BLOCK), -1.0, F32)
        numbers = [vi[k, batch : batch + 1, :] for k in range(top)]
        named = jnp.zeros((experts, BLOCK), F32)
        for number in numbers:
            named = named + jnp.where(number == name, 1.0, 0.0)
        before = jnp.dot(named.astype(BF16), earlier, preferred_element_type=F32)
        for k, number in enumerate(numbers):
            slot = jnp.sum(jnp.where(number == name, before, 0.0), axis=0, keepdims=True)
            meta[batch, 0, k : k + 1, :BLOCK] = number.astype(F32) * SLOTS + slot
            meta[batch, 0, 8 + k : 9 + k, :BLOCK] = vw[k, batch : batch + 1, :]

    entries = w_mod.shape[1] // 2
    level = jnp.concatenate([vl[0:1, :], vl[1:2, :]], axis=1).astype(F32)
    level = jnp.broadcast_to(level, (2 * BLOCK, 2 * BLOCK)).T
    index = lax.broadcasted_iota(jnp.int32, (1, entries), 1).astype(F32)
    angles = level * jnp.exp(-math.log(10000.0) * index / entries)
    embed = jnp.concatenate([jnp.cos(angles), jnp.sin(angles)], axis=1).astype(BF16)
    loads[3].wait()
    mod[...] = jnp.dot(embed, vm[...], preferred_element_type=F32)

    def tell(batch, p):
        return remote(
            meta.at[batch, 0], meta.at[batch, p], m_send.at[batch, p - 1], m_recv.at[batch, p - 1],
            along(batch, OFFSET[p], 0, 0),
        )

    for batch in range(2):
        for p in (1, 2, 3):
            tell(batch, p).start()

    def spread(batch, part, way):
        rows = pl.ds(part * PIECE, PIECE)
        return remote(
            gathered.at[batch, 0, rows], gathered.at[batch, 1 + way, rows],
            g_send.at[batch, way, part], g_recv.at[batch, way, part], along(batch, 1 - 2 * way, 0, 0),
        )

    def normalize(batch, part):
        rows = pl.ds(part * PIECE, PIECE)
        got(arrived.at[batch, rows], z_recv.at[batch + 2 * part])
        values = arrived[batch, rows, :].astype(F32)
        mean_square = jnp.mean(values * values, axis=1, keepdims=True)
        own = pl.ds(batch * BLOCK + part * PIECE, PIECE)
        normed = values * lax.rsqrt(mean_square + epsilon) * (1.0 + mod[own, :features]) + mod[own, features:]
        gathered[batch, 0, rows, :] = normed.astype(BF16)
        spread(batch, part, 0).start()
        spread(batch, part, 1).start()

    def spread_in(batch, way, half):
        for part in (2 * half, 2 * half + 1):
            got(gathered.at[batch, 1 + way, pl.ds(part * PIECE, PIECE)], g_recv.at[batch, way, part])

    def hand_on(batch, way):
        rows = pl.ds(way * HALF, HALF)
        return remote(
            gathered.at[batch, 1 + way, rows], gathered.at[batch, 3, rows],
            gf_send.at[batch, way], gf_recv.at[batch, way], along(batch, 1 - 2 * way, 0, 0),
        )

    def forward(batch, way):
        spread_in(batch, way, way)
        hand_on(batch, way).start()

    pick = lax.broadcasted_iota(jnp.int32, (PICKS, 2 * BLOCK), 0)
    far, other_seat, slot_of = pick // (2 * SLOTS), (pick // SLOTS) % 2, pick % SLOTS
    seat_of = core + other_seat * (1 - 2 * core)
    wanted = []
    for batch in range(2):
        if batch == 0:
            line = x * 8 + ((y + far) % SIDE) * 2
        else:
            line = ((x + far) % SIDE) * 8 + y * 2
        wanted.append(((line + seat_of) * SLOTS + slot_of).astype(F32))

    def exchange(p, batch, block):
        step, other = block // 2, block % 2
        if step == 2:
            return remote(
                picked.at[p, batch, block], passed.at[p, batch, other], b_send.at[p, batch], f_recv.at[p, batch],
                along(batch, 0, 1 - 2 * other, 0),
            )
        return remote(
            picked.at[p, batch, block], rows_in.at[p, batch, block], b_send.at[p, batch], b_recv.at[p, batch],
            along(batch, 0, step, other),
        )

    order = (4, 5, 2, 6, 3, 7, 1)

    def select(batch, p):
        if p == 3:
            for way in range(2):
                got(gathered.at[batch, 3, pl.ds(way * HALF, HALF)], gf_recv.at[batch, way])
        elif p:
            spread_in(batch, p - 1, 2 - p)
        if p:
            got(meta.at[batch, p], m_recv.at[batch, p - 1])
        hit = jnp.zeros((PICKS, 2 * BLOCK), F32)
        worth = jnp.zeros((PICKS, 2 * BLOCK), F32)
        for k in range(top):
            same = meta[batch, p, k : k + 1, :] == wanted[batch]
            hit = jnp.where(same, 1.0, hit)
            worth = jnp.where(same, meta[batch, p, 8 + k : 9 + k, :], worth)
        chosen = jnp.dot(hit[:, :BLOCK].astype(BF16), gathered[batch, p], preferred_element_type=F32)
        chosen = chosen.astype(BF16).reshape(2 * SIDE, SLOTS, features)
        picked[p, batch] = chosen
        rows_in[p, batch, 0] = chosen[0]
        for block in order:
            exchange(p, batch, block).start()
        worth = worth.T
        high = worth[:BLOCK].astype(BF16)
        weigh[batch, p, :BLOCK, :] = high
        weigh[batch, p, BLOCK:, :] = (worth[:BLOCK] - high.astype(F32)).astype(BF16)

    def pass_on(p, batch):
        return [
            remote(
                passed.at[p, batch, other], rows_in.at[p, batch, 4 + other], f_send.at[p, batch], b_recv.at[p, batch],
                along(batch, 0, 1 - 2 * other, other),
            )
            for other in range(2)
        ]

    def move_on(p, batch):
        got(passed.at[p, batch], f_recv.at[p, batch])
        for copy in pass_on(p, batch):
            copy.start()

    for part in (0, 1):
        for batch in range(2):
            normalize(batch, part)
    normalize(0, 2)
    forward(0, 0)
    normalize(1, 2)
    forward(1, 0)
    normalize(0, 3)
    select(0, 0)
    normalize(1, 3)
    select(1, 0)
    forward(0, 1)
    forward(1, 1)
    move_on(0, 0)
    move_on(0, 1)
    select(0, 1)
    select(1, 1)
    select(0, 2)
    select(1, 2)
    move_on(1, 0)
    move_on(1, 1)
    select(0, 3)
    select(1, 3)
    move_on(2, 0)
    move_on(2, 1)

    for load in loads[4:]:
        load.wait()

    def back(p, batch, block):
        step, other = block // 2, block % 2
        if step == 2:
            return remote(
                rows_out.at[p, batch, block], passed_back.at[p, batch, other], o_send.at[p, batch],
                p_recv.at[p, batch], along(batch, 0, 2 * other - 1, 0),
            )
        return remote(
            rows_out.at[p, batch, block], returned.at[p, batch, block], o_send.at[p, batch], o_recv.at[p, batch],
            along(batch, 0, 4 - step, other),
        )

    def pass_back(p, batch):
        return [
            remote(
                passed_back.at[p, batch, other], returned.at[p, batch, 4 + other], p_send.at[p, batch],
                o_recv.at[p, batch], along(batch, 0, 2 * other - 1, other),
            )
            for other in range(2)
        ]

    def move_back(p):
        for batch in range(2):
            got(passed_back.at[p, batch], p_recv.at[p, batch])
            for copy in pass_back(p, batch):
                copy.start()

    def send_back(p):
        for block in order:
            for batch in range(2):
                back(p, batch, block).start()

    def work(p, carry):
        @pl.when(p == 1)
        def _():
            move_on(3, 0)
            move_on(3, 1)

        for batch in range(2):
            got(rows_in.at[p, batch, pl.ds(1, 7)], b_recv.at[p, batch])
        rows = rows_in[p].reshape(2 * PICKS, features)
        gate_part = jnp.dot(rows, vg[...], preferred_element_type=F32)
        up_part = jnp.dot(rows, vu[...], preferred_element_type=F32)
        hidden = (gate_part / (1.0 + jnp.exp(-gate_part)) * up_part).astype(BF16)
        produced = jnp.dot(hidden, vd[...], preferred_element_type=F32).astype(BF16)
        produced = produced.reshape(2, 2 * SIDE, SLOTS, features)
        rows_out[p] = produced
        for batch in range(2):
            returned[p, batch, 0] = produced[batch, 0]

        @pl.when(p > 1)
        def _():
            move_back(p - 1)

        @pl.when(p > 0)
        def _():
            send_back(p)

        return carry

    lax.fori_loop(0, SIDE, work, 0)

    def add_up(p, batch):
        got(returned.at[p, batch, pl.ds(1, 7)], o_recv.at[p, batch])
        rows = returned[p, batch].reshape(PICKS, features)
        both = jnp.dot(weigh[batch, p], rows, preferred_element_type=F32)
        return both[:BLOCK] + both[BLOCK:]

    def sum_half(batch, way):
        return remote(
            far_part.at[batch, way], half_in.at[batch, way], h_send.at[batch, way], h_recv.at[batch, way],
            along(batch, 2 * way - 1, 0, 0),
        )

    def sum_home(batch, way, part):
        return remote(
            near_part.at[batch, way, part], part_in.at[batch, way, part], q_send.at[batch, way, part],
            q_recv.at[batch, way, part], along(batch, 2 * way - 1, 0, 0),
        )

    def add_own(batch, carry):
        total[batch] = add_up(0, batch) + arrived[batch].astype(F32)
        return carry

    def add_near(way):
        def add(batch, carry):
            near = add_up(1 + way, batch).reshape(2, HALF, features)
            near_held[batch, way] = near[way]
            near_part[batch, way, 1 - way] = near[1 - way].astype(BF16)
            sum_home(batch, way, 1 - way).start()
            return carry

        return add

    def add_far(batch, carry):
        far_part[batch] = add_up(3, batch).astype(BF16).reshape(2, HALF, features)
        sum_half(batch, 0).start()
        sum_half(batch, 1).start()
        return carry

    lax.fori_loop(0, 2, add_near(0), 0)
    move_back(3)
    send_back(0)
    lax.fori_loop(0, 2, add_near(1), 0)
    lax.fori_loop(0, 2, add_far, 0)
    move_back(0)

    def add_half(batch, carry):
        for way in range(2):
            got(half_in.at[batch, way], h_recv.at[batch, way])
            near_part[batch, way, way] = (near_held[batch, way] + half_in[batch, way].astype(F32)).astype(BF16)
            sum_home(batch, way, way).start()
        return carry

    lax.fori_loop(0, 2, add_half, 0)
    lax.fori_loop(0, 2, add_own, 0)

    def finish(batch, carry):
        for part in range(2):
            for way in range(2):
                got(part_in.at[batch, way, part], q_recv.at[batch, way, part])
            rows = pl.ds(part * HALF, HALF)
            sums = part_in[batch, 0, part].astype(F32) + part_in[batch, 1, part].astype(F32)
            out[batch, rows, :] = (total[batch, rows, :] + sums).astype(BF16)
        return carry

    lax.fori_loop(0, 2, finish, 0)

    for piece in range(8):
        shift(piece).wait_send()
    for batch in range(2):
        for p in (1, 2, 3):
            tell(batch, p).wait_send()
        for way in range(2):
            for part in range(4):
                spread(batch, part, way).wait_send()
            hand_on(batch, way).wait_send()
            sum_half(batch, way).wait_send()
            sum_home(batch, way, 0).wait_send()
            sum_home(batch, way, 1).wait_send()
        for p in range(SIDE):
            left(picked.at[p, batch, pl.ds(1, 7)], b_send.at[p, batch])
            left(passed.at[p, batch], f_send.at[p, batch])
            left(rows_out.at[p, batch, pl.ds(1, 7)], o_send.at[p, batch])
            left(passed_back.at[p, batch], p_send.at[p, batch])


def shards(emitted, levels, expert_ids, gate_values, w_gate, w_up, w_down, w_mod):
    batches, rows, features = emitted.shape[1:]
    top, inner = expert_ids.shape[3], w_gate.shape[3]
    tokens = batches * rows
    ids = expert_ids.transpose(0, 3, 1, 2)
    gates = gate_values.transpose(0, 3, 1, 2)
    anywhere, vmem = pl.BlockSpec(memory_space=pl.ANY), pl.BlockSpec(memory_space=pltpu.VMEM)
    dma = pltpu.SemaphoreType.DMA
    lines = pltpu.VMEM((SIDE, 2, 2 * SIDE, SLOTS, features), BF16)
    out = pl.pallas_call(
        functools.partial(layer_kernel, lax.axis_size("section"), top),
        out_shape=jax.ShapeDtypeStruct((batches, rows, features), BF16),
        in_specs=[anywhere] * 8,
        out_specs=vmem,
        scratch_shapes=[
            pltpu.VMEM((features, inner), BF16),
            pltpu.VMEM((features, inner), BF16),
            pltpu.VMEM((inner, features), BF16),
            pltpu.VMEM(w_mod.shape[1:], BF16),
            pltpu.VMEM((batches, rows), jnp.int32),
            pltpu.VMEM((top, batches, rows), jnp.int32),
            pltpu.VMEM((top, batches, rows), F32),
            pltpu.VMEM((tokens, 2 * features), F32),
            pltpu.VMEM((2, SIDE, 16, 2 * BLOCK), F32),
            pltpu.VMEM((2, SIDE, 2 * BLOCK, PICKS), BF16),
            pltpu.VMEM((2, BLOCK, features), BF16),
            pltpu.VMEM((2, SIDE, BLOCK, features), BF16),
            lines,
            pltpu.VMEM((SIDE, 2, 2, SLOTS, features), BF16),
            lines,
            lines,
            pltpu.VMEM((SIDE, 2, 2, SLOTS, features), BF16),
            lines,
            pltpu.VMEM((2, 2, HALF, features), BF16),
            pltpu.VMEM((2, 2, 2, HALF, features), BF16),
            pltpu.VMEM((2, 2, HALF, features), F32),
            pltpu.VMEM((2, 2, HALF, features), BF16),
            pltpu.VMEM((2, 2, 2, HALF, features), BF16),
            pltpu.VMEM((2, BLOCK, features), F32),
            dma((7,)), dma((8,)), dma((8,)),
            dma((2, 3)), dma((2, 3)),
            dma((2, 2, 4)), dma((2, 2, 4)), dma((2, 2)), dma((2, 2)),
            dma((SIDE, 2)), dma((SIDE, 2)), dma((SIDE, 2)), dma((SIDE, 2)),
            dma((SIDE, 2)), dma((SIDE, 2)), dma((SIDE, 2)), dma((SIDE, 2)),
            dma((2, 2)), dma((2, 2)), dma((2, 2, 2)), dma((2, 2, 2)),
        ],
        compiler_params=pltpu.CompilerParams(
            collective_id=0, has_side_effects=True, vmem_limit_bytes=60 * 1024 * 1024
        ),
    )(emitted, levels, ids, gates, w_gate, w_up, w_down, w_mod)
    return out[None]


def solution(mesh):
    placed = (
        P("section", None, "expert", None),
        P("section", None, "expert"),
        P("section", None, "expert", None),
        P("section", None, "expert", None),
        P("section", "expert", None, None),
        P("section", "expert", None, None),
        P("section", "expert", None, None),
        P("section", None, None),
    )
    return jax.shard_map(
        shards,
        mesh=mesh,
        in_specs=placed,
        out_specs=P("section", None, "expert", None),
        check_vma=False,
    )
```

```python
import functools
import math

import jax
import jax.numpy as jnp
from jax import lax
from jax.experimental import pallas as pl
from jax.experimental.pallas import tpu as pltpu
from jax.sharding import PartitionSpec as P

epsilon = 1e-06
MESH = pl.DeviceIdType.MESH
F32, BF16 = jnp.float32, jnp.bfloat16
SIDE = 4
SLOTS = 16
BLOCK = 64
HALF = BLOCK // 2
PIECE = BLOCK // 4
OFFSET = (0, 1, 3, 2)
PICKS = SIDE * 2 * SLOTS


def layer_kernel(
    sections, top,
    emitted, levels, ids, gates, w_gate, w_up, w_down, w_mod,
    out,
    vg, vu, vd, vm, vl, vi, vw, mod, meta, weigh,
    arrived, gathered, picked, passed, rows_in, rows_out, passed_back, returned,
    far_part, near_part, near_held, half_in, part_in, total,
    load_sem, z_send, z_recv, m_send, m_recv, g_send, g_recv, gf_send, gf_recv,
    b_send, b_recv, f_recv, f_send, o_send, o_recv, p_recv, p_send, h_send, h_recv, q_send, q_recv,
):
    section = lax.axis_index("section")
    place = lax.axis_index("expert")
    x, y, core = place // 8, (place // 2) % SIDE, place % 2
    features = arrived.shape[2]

    def at(dx, dy, other):
        seat = core + other * (1 - 2 * core)
        return (section, ((x + dx + 8) % SIDE) * 8 + ((y + dy + 8) % SIDE) * 2 + seat)

    def along(batch, da, db, other):
        return at(da + batch * (db - da), db + batch * (da - db), other)

    def remote(src, dst, send, recv, device):
        return pltpu.make_async_remote_copy(
            src_ref=src, dst_ref=dst, send_sem=send, recv_sem=recv, device_id=device, device_id_type=MESH
        )

    def got(dst, recv):
        remote(dst, dst, recv, recv, (section, place)).wait_recv()

    def left(src, send):
        remote(src, src, send, send, (section, place)).wait_send()

    after = ((section + 1) % sections, place)
    ahead = ((section + sections - 1) % sections, place)

    barrier = pltpu.get_barrier_semaphore()
    friends = [after, ahead, at(0, 0, 1), at(2, 0, 0), at(0, 2, 0)]
    for step in (1, -1):
        for other in (0, 1):
            friends += [at(step, 0, other), at(0, step, other)]
    for friend in friends:
        pl.semaphore_signal(barrier, inc=1, device_id=friend, device_id_type=MESH)

    sources = (levels.at[0], ids.at[0], gates.at[0], w_mod.at[0], w_gate.at[0, 0], w_up.at[0, 0], w_down.at[0, 0])
    targets = (vl, vi, vw, vm, vg, vu, vd)
    loads = [pltpu.make_async_copy(a, b, load_sem.at[i]) for i, (a, b) in enumerate(zip(sources, targets))]
    for load in loads[:4]:
        load.start()
    pl.semaphore_wait(barrier, len(friends))

    def shift(piece):
        batch, rows = piece % 2, pl.ds((piece // 2) * PIECE, PIECE)
        return remote(
            emitted.at[0, batch, rows], arrived.at[batch, rows], z_send.at[piece], z_recv.at[piece], after
        )

    for piece in range(8):
        shift(piece).start()
    for load in loads[4:]:
        load.start()

    for load in loads[:3]:
        load.wait()

    experts = SIDE * SIDE * 2
    name = lax.broadcasted_iota(jnp.int32, (experts, BLOCK), 0)
    row = lax.broadcasted_iota(jnp.int32, (BLOCK, BLOCK), 0)
    col = lax.broadcasted_iota(jnp.int32, (BLOCK, BLOCK), 1)
    earlier = jnp.where(row < col, 1.0, 0.0).astype(BF16)
    for batch in range(2):
        meta[batch, 0] = jnp.full((16, 2 * BLOCK), -1.0, F32)
        numbers = [vi[k, batch : batch + 1, :] for k in range(top)]
        named = jnp.zeros((experts, BLOCK), F32)
        for number in numbers:
            named = named + jnp.where(number == name, 1.0, 0.0)
        before = jnp.dot(named.astype(BF16), earlier, preferred_element_type=F32)
        for k, number in enumerate(numbers):
            slot = jnp.sum(jnp.where(number == name, before, 0.0), axis=0, keepdims=True)
            meta[batch, 0, k : k + 1, :BLOCK] = number.astype(F32) * SLOTS + slot
            meta[batch, 0, 8 + k : 9 + k, :BLOCK] = vw[k, batch : batch + 1, :]

    entries = w_mod.shape[1] // 2
    level = jnp.concatenate([vl[0:1, :], vl[1:2, :]], axis=1).astype(F32)
    level = jnp.broadcast_to(level, (2 * BLOCK, 2 * BLOCK)).T
    index = lax.broadcasted_iota(jnp.int32, (1, entries), 1).astype(F32)
    angles = level * jnp.exp(-math.log(10000.0) * index / entries)
    embed = jnp.concatenate([jnp.cos(angles), jnp.sin(angles)], axis=1).astype(BF16)
    loads[3].wait()
    mod[...] = jnp.dot(embed, vm[...], preferred_element_type=F32)

    def tell(batch, p):
        return remote(
            meta.at[batch, 0], meta.at[batch, p], m_send.at[batch, p - 1], m_recv.at[batch, p - 1],
            along(batch, OFFSET[p], 0, 0),
        )

    for batch in range(2):
        for p in (1, 2, 3):
            tell(batch, p).start()

    def spread(batch, part, way):
        rows = pl.ds(part * PIECE, PIECE)
        return remote(
            gathered.at[batch, 0, rows], gathered.at[batch, 1 + way, rows],
            g_send.at[batch, way, part], g_recv.at[batch, way, part], along(batch, 1 - 2 * way, 0, 0),
        )

    def normalize(batch, part):
        rows = pl.ds(part * PIECE, PIECE)
        got(arrived.at[batch, rows], z_recv.at[batch + 2 * part])
        values = arrived[batch, rows, :].astype(F32)
        mean_square = jnp.mean(values * values, axis=1, keepdims=True)
        own = pl.ds(batch * BLOCK + part * PIECE, PIECE)
        normed = values * lax.rsqrt(mean_square + epsilon) * (1.0 + mod[own, :features]) + mod[own, features:]
        gathered[batch, 0, rows, :] = normed.astype(BF16)
        spread(batch, part, 0).start()
        spread(batch, part, 1).start()

    def spread_in(batch, way, half):
        for part in (2 * half, 2 * half + 1):
            got(gathered.at[batch, 1 + way, pl.ds(part * PIECE, PIECE)], g_recv.at[batch, way, part])

    def hand_on(batch, way):
        rows = pl.ds(way * HALF, HALF)
        return remote(
            gathered.at[batch, 1 + way, rows], gathered.at[batch, 3, rows],
            gf_send.at[batch, way], gf_recv.at[batch, way], along(batch, 1 - 2 * way, 0, 0),
        )

    def forward(batch, way):
        spread_in(batch, way, way)
        hand_on(batch, way).start()

    pick = lax.broadcasted_iota(jnp.int32, (PICKS, 2 * BLOCK), 0)
    far, other_seat, slot_of = pick // (2 * SLOTS), (pick // SLOTS) % 2, pick % SLOTS
    seat_of = core + other_seat * (1 - 2 * core)
    wanted = []
    for batch in range(2):
        if batch == 0:
            line = x * 8 + ((y + far) % SIDE) * 2
        else:
            line = ((x + far) % SIDE) * 8 + y * 2
        wanted.append(((line + seat_of) * SLOTS + slot_of).astype(F32))

    def exchange(p, batch, block):
        step, other = block // 2, block % 2
        if step == 2:
            return remote(
                picked.at[p, batch, block], passed.at[p, batch, other], b_send.at[p, batch], f_recv.at[p, batch],
                along(batch, 0, 1 - 2 * other, 0),
            )
        return remote(
            picked.at[p, batch, block], rows_in.at[p, batch, block], b_send.at[p, batch], b_recv.at[p, batch],
            along(batch, 0, step, other),
        )

    order = (4, 5, 2, 6, 3, 7, 1)

    def select(batch, p):
        if p == 3:
            for way in range(2):
                got(gathered.at[batch, 3, pl.ds(way * HALF, HALF)], gf_recv.at[batch, way])
        elif p:
            spread_in(batch, p - 1, 2 - p)
        if p:
            got(meta.at[batch, p], m_recv.at[batch, p - 1])
        hit = jnp.zeros((PICKS, 2 * BLOCK), F32)
        worth = jnp.zeros((PICKS, 2 * BLOCK), F32)
        for k in range(top):
            same = meta[batch, p, k : k + 1, :] == wanted[batch]
            hit = jnp.where(same, 1.0, hit)
            worth = jnp.where(same, meta[batch, p, 8 + k : 9 + k, :], worth)
        chosen = jnp.dot(hit[:, :BLOCK].astype(BF16), gathered[batch, p], preferred_element_type=F32)
        chosen = chosen.astype(BF16).reshape(2 * SIDE, SLOTS, features)
        picked[p, batch] = chosen
        rows_in[p, batch, 0] = chosen[0]
        for block in order:
            exchange(p, batch, block).start()
        worth = worth.T
        high = worth[:BLOCK].astype(BF16)
        weigh[batch, p, :BLOCK, :] = high
        weigh[batch, p, BLOCK:, :] = (worth[:BLOCK] - high.astype(F32)).astype(BF16)

    def pass_on(p, batch):
        return [
            remote(
                passed.at[p, batch, other], rows_in.at[p, batch, 4 + other], f_send.at[p, batch], b_recv.at[p, batch],
                along(batch, 0, 1 - 2 * other, other),
            )
            for other in range(2)
        ]

    def move_on(p, batch):
        got(passed.at[p, batch], f_recv.at[p, batch])
        for copy in pass_on(p, batch):
            copy.start()

    for part in (0, 1):
        for batch in range(2):
            normalize(batch, part)
    normalize(0, 2)
    forward(0, 0)
    normalize(1, 2)
    forward(1, 0)
    normalize(0, 3)
    normalize(1, 3)
    select(0, 0)
    select(1, 0)
    forward(0, 1)
    forward(1, 1)
    move_on(0, 0)
    move_on(0, 1)
    select(0, 1)
    select(1, 1)
    select(0, 2)
    select(1, 2)
    move_on(1, 0)
    move_on(1, 1)
    select(0, 3)
    select(1, 3)
    move_on(2, 0)
    move_on(2, 1)

    for load in loads[4:]:
        load.wait()

    def back(p, batch, block):
        step, other = block // 2, block % 2
        if step == 2:
            return remote(
                rows_out.at[p, batch, block], passed_back.at[p, batch, other], o_send.at[p, batch],
                p_recv.at[p, batch], along(batch, 0, 2 * other - 1, 0),
            )
        return remote(
            rows_out.at[p, batch, block], returned.at[p, batch, block], o_send.at[p, batch], o_recv.at[p, batch],
            along(batch, 0, 4 - step, other),
        )

    def pass_back(p, batch):
        return [
            remote(
                passed_back.at[p, batch, other], returned.at[p, batch, 4 + other], p_send.at[p, batch],
                o_recv.at[p, batch], along(batch, 0, 2 * other - 1, other),
            )
            for other in range(2)
        ]

    def move_back(p):
        for batch in range(2):
            got(passed_back.at[p, batch], p_recv.at[p, batch])
            for copy in pass_back(p, batch):
                copy.start()

    def send_back(p):
        for block in order:
            for batch in range(2):
                back(p, batch, block).start()

    def work(p, carry):
        @pl.when(p == 1)
        def _():
            move_on(3, 0)
            move_on(3, 1)

        for batch in range(2):
            got(rows_in.at[p, batch, pl.ds(1, 7)], b_recv.at[p, batch])
        rows = rows_in[p].reshape(2 * PICKS, features)
        gate_part = jnp.dot(rows, vg[...], preferred_element_type=F32)
        up_part = jnp.dot(rows, vu[...], preferred_element_type=F32)
        hidden = (gate_part / (1.0 + jnp.exp(-gate_part)) * up_part).astype(BF16)
        produced = jnp.dot(hidden, vd[...], preferred_element_type=F32).astype(BF16)
        produced = produced.reshape(2, 2 * SIDE, SLOTS, features)
        rows_out[p] = produced
        for batch in range(2):
            returned[p, batch, 0] = produced[batch, 0]

        @pl.when(p > 1)
        def _():
            move_back(p - 1)

        @pl.when(p > 0)
        def _():
            send_back(p)

        return carry

    lax.fori_loop(0, SIDE, work, 0)

    def add_up(p, batch):
        got(returned.at[p, batch, pl.ds(1, 7)], o_recv.at[p, batch])
        rows = returned[p, batch].reshape(PICKS, features)
        both = jnp.dot(weigh[batch, p], rows, preferred_element_type=F32)
        return both[:BLOCK] + both[BLOCK:]

    def sum_half(batch, way):
        return remote(
            far_part.at[batch, way], half_in.at[batch, way], h_send.at[batch, way], h_recv.at[batch, way],
            along(batch, 2 * way - 1, 0, 0),
        )

    def sum_home(batch, way, part):
        return remote(
            near_part.at[batch, way, part], part_in.at[batch, way, part], q_send.at[batch, way, part],
            q_recv.at[batch, way, part], along(batch, 2 * way - 1, 0, 0),
        )

    def add_own(batch, carry):
        total[batch] = add_up(0, batch) + arrived[batch].astype(F32)
        return carry

    def add_near(way):
        def add(batch, carry):
            near = add_up(1 + way, batch).reshape(2, HALF, features)
            near_held[batch, way] = near[way]
            near_part[batch, way, 1 - way] = near[1 - way].astype(BF16)
            sum_home(batch, way, 1 - way).start()
            return carry

        return add

    def add_far(batch, carry):
        far_part[batch] = add_up(3, batch).astype(BF16).reshape(2, HALF, features)
        sum_half(batch, 0).start()
        sum_half(batch, 1).start()
        return carry

    lax.fori_loop(0, 2, add_near(0), 0)
    move_back(3)
    send_back(0)
    lax.fori_loop(0, 2, add_near(1), 0)
    lax.fori_loop(0, 2, add_far, 0)
    move_back(0)

    def add_half(batch, carry):
        for way in range(2):
            got(half_in.at[batch, way], h_recv.at[batch, way])
            near_part[batch, way, way] = (near_held[batch, way] + half_in[batch, way].astype(F32)).astype(BF16)
            sum_home(batch, way, way).start()
        return carry

    lax.fori_loop(0, 2, add_half, 0)
    lax.fori_loop(0, 2, add_own, 0)

    def finish(batch, carry):
        for part in range(2):
            for way in range(2):
                got(part_in.at[batch, way, part], q_recv.at[batch, way, part])
            rows = pl.ds(part * HALF, HALF)
            sums = part_in[batch, 0, part].astype(F32) + part_in[batch, 1, part].astype(F32)
            out[batch, rows, :] = (total[batch, rows, :] + sums).astype(BF16)
        return carry

    lax.fori_loop(0, 2, finish, 0)

    for piece in range(8):
        shift(piece).wait_send()
    for batch in range(2):
        for p in (1, 2, 3):
            tell(batch, p).wait_send()
        for way in range(2):
            for part in range(4):
                spread(batch, part, way).wait_send()
            hand_on(batch, way).wait_send()
            sum_half(batch, way).wait_send()
            sum_home(batch, way, 0).wait_send()
            sum_home(batch, way, 1).wait_send()
        for p in range(SIDE):
            left(picked.at[p, batch, pl.ds(1, 7)], b_send.at[p, batch])
            left(passed.at[p, batch], f_send.at[p, batch])
            left(rows_out.at[p, batch, pl.ds(1, 7)], o_send.at[p, batch])
            left(passed_back.at[p, batch], p_send.at[p, batch])


def shards(emitted, levels, expert_ids, gate_values, w_gate, w_up, w_down, w_mod):
    batches, rows, features = emitted.shape[1:]
    top, inner = expert_ids.shape[3], w_gate.shape[3]
    tokens = batches * rows
    ids = expert_ids.transpose(0, 3, 1, 2)
    gates = gate_values.transpose(0, 3, 1, 2)
    anywhere, vmem = pl.BlockSpec(memory_space=pl.ANY), pl.BlockSpec(memory_space=pltpu.VMEM)
    dma = pltpu.SemaphoreType.DMA
    lines = pltpu.VMEM((SIDE, 2, 2 * SIDE, SLOTS, features), BF16)
    held = [
        pltpu.with_memory_space_constraint(array, pltpu.HBM)
        for array in (emitted, levels, ids, gates, w_gate, w_up, w_down, w_mod)
    ]
    out = pl.pallas_call(
        functools.partial(layer_kernel, lax.axis_size("section"), top),
        out_shape=jax.ShapeDtypeStruct((batches, rows, features), BF16),
        in_specs=[anywhere] * 8,
        out_specs=vmem,
        scratch_shapes=[
            pltpu.VMEM((features, inner), BF16),
            pltpu.VMEM((features, inner), BF16),
            pltpu.VMEM((inner, features), BF16),
            pltpu.VMEM(w_mod.shape[1:], BF16),
            pltpu.VMEM((batches, rows), jnp.int32),
            pltpu.VMEM((top, batches, rows), jnp.int32),
            pltpu.VMEM((top, batches, rows), F32),
            pltpu.VMEM((tokens, 2 * features), F32),
            pltpu.VMEM((2, SIDE, 16, 2 * BLOCK), F32),
            pltpu.VMEM((2, SIDE, 2 * BLOCK, PICKS), BF16),
            pltpu.VMEM((2, BLOCK, features), BF16),
            pltpu.VMEM((2, SIDE, BLOCK, features), BF16),
            lines,
            pltpu.VMEM((SIDE, 2, 2, SLOTS, features), BF16),
            lines,
            lines,
            pltpu.VMEM((SIDE, 2, 2, SLOTS, features), BF16),
            lines,
            pltpu.VMEM((2, 2, HALF, features), BF16),
            pltpu.VMEM((2, 2, 2, HALF, features), BF16),
            pltpu.VMEM((2, 2, HALF, features), F32),
            pltpu.VMEM((2, 2, HALF, features), BF16),
            pltpu.VMEM((2, 2, 2, HALF, features), BF16),
            pltpu.VMEM((2, BLOCK, features), F32),
            dma((7,)), dma((8,)), dma((8,)),
            dma((2, 3)), dma((2, 3)),
            dma((2, 2, 4)), dma((2, 2, 4)), dma((2, 2)), dma((2, 2)),
            dma((SIDE, 2)), dma((SIDE, 2)), dma((SIDE, 2)), dma((SIDE, 2)),
            dma((SIDE, 2)), dma((SIDE, 2)), dma((SIDE, 2)), dma((SIDE, 2)),
            dma((2, 2)), dma((2, 2)), dma((2, 2, 2)), dma((2, 2, 2)),
        ],
        compiler_params=pltpu.CompilerParams(
            collective_id=0, has_side_effects=True, vmem_limit_bytes=52 * 1024 * 1024
        ),
    )(*held)
    return out[None]


def solution(mesh):
    placed = (
        P("section", None, "expert", None),
        P("section", None, "expert"),
        P("section", None, "expert", None),
        P("section", None, "expert", None),
        P("section", "expert", None, None),
        P("section", "expert", None, None),
        P("section", "expert", None, None),
        P("section", None, None),
    )
    return jax.shard_map(
        shards,
        mesh=mesh,
        in_specs=placed,
        out_specs=P("section", None, "expert", None),
        check_vma=False,
    )
```

```python
import functools
import math

import jax
import jax.numpy as jnp
from jax import lax
from jax.experimental import pallas as pl
from jax.experimental.pallas import tpu as pltpu
from jax.sharding import PartitionSpec as P

epsilon = 1e-06
MESH = pl.DeviceIdType.MESH
F32, BF16 = jnp.float32, jnp.bfloat16
SIDE = 4
SLOTS = 16
BLOCK = 64
HALF = BLOCK // 2
PIECE = BLOCK // 4
OFFSET = (0, 1, 3, 2)
PICKS = SIDE * 2 * SLOTS


def layer_kernel(
    sections, top,
    emitted, levels, ids, gates, w_gate, w_up, w_down, w_mod,
    out,
    vg, vu, vd, vm, vl, vi, vw, mod, meta, weigh,
    arrived, gathered, picked, passed, rows_in, rows_out, passed_back, returned,
    far_part, near_part, near_held, half_in, part_in, total,
    load_sem, z_send, z_recv, m_send, m_recv, g_send, g_recv, gf_send, gf_recv,
    b_send, b_recv, f_recv, f_send, o_send, o_recv, p_recv, p_send, h_send, h_recv, q_send, q_recv,
):
    section = lax.axis_index("section")
    place = lax.axis_index("expert")
    x, y, core = place // 8, (place // 2) % SIDE, place % 2
    features = arrived.shape[2]

    def at(dx, dy, other):
        seat = core + other * (1 - 2 * core)
        return (section, ((x + dx + 8) % SIDE) * 8 + ((y + dy + 8) % SIDE) * 2 + seat)

    def along(batch, da, db, other):
        return at(da + batch * (db - da), db + batch * (da - db), other)

    def remote(src, dst, send, recv, device):
        return pltpu.make_async_remote_copy(
            src_ref=src, dst_ref=dst, send_sem=send, recv_sem=recv, device_id=device, device_id_type=MESH
        )

    def got(dst, recv):
        remote(dst, dst, recv, recv, (section, place)).wait_recv()

    def left(src, send):
        remote(src, src, send, send, (section, place)).wait_send()

    after = ((section + 1) % sections, place)
    ahead = ((section + sections - 1) % sections, place)

    barrier = pltpu.get_barrier_semaphore()
    friends = [after, ahead, at(0, 0, 1)]
    for step in (1, -1):
        for other in (0, 1):
            friends += [at(step, 0, other), at(0, step, other)]
    for friend in friends:
        pl.semaphore_signal(barrier, inc=1, device_id=friend, device_id_type=MESH)

    sources = (levels.at[0], ids.at[0], gates.at[0], w_mod.at[0], w_gate.at[0, 0], w_up.at[0, 0], w_down.at[0, 0])
    targets = (vl, vi, vw, vm, vg, vu, vd)
    loads = [pltpu.make_async_copy(a, b, load_sem.at[i]) for i, (a, b) in enumerate(zip(sources, targets))]
    pl.semaphore_wait(barrier, len(friends))

    def shift(piece):
        batch, rows = piece % 2, pl.ds((piece // 2) * PIECE, PIECE)
        return remote(
            emitted.at[0, batch, rows], arrived.at[batch, rows], z_send.at[piece], z_recv.at[piece], after
        )

    for piece in range(8):
        shift(piece).start()
    for load in loads:
        load.start()

    for load in loads[:3]:
        load.wait()

    experts = SIDE * SIDE * 2
    name = lax.broadcasted_iota(jnp.int32, (experts, BLOCK), 0)
    row = lax.broadcasted_iota(jnp.int32, (BLOCK, BLOCK), 0)
    col = lax.broadcasted_iota(jnp.int32, (BLOCK, BLOCK), 1)
    earlier = jnp.where(row < col, 1.0, 0.0).astype(BF16)
    for batch in range(2):
        meta[batch, 0] = jnp.full((16, 2 * BLOCK), -1.0, F32)
        numbers = [vi[k, batch : batch + 1, :] for k in range(top)]
        named = jnp.zeros((experts, BLOCK), F32)
        for number in numbers:
            named = named + jnp.where(number == name, 1.0, 0.0)
        before = jnp.dot(named.astype(BF16), earlier, preferred_element_type=F32)
        for k, number in enumerate(numbers):
            slot = jnp.sum(jnp.where(number == name, before, 0.0), axis=0, keepdims=True)
            meta[batch, 0, k : k + 1, :BLOCK] = number.astype(F32) * SLOTS + slot
            meta[batch, 0, 8 + k : 9 + k, :BLOCK] = vw[k, batch : batch + 1, :]

    entries = w_mod.shape[1] // 2
    level = jnp.concatenate([vl[0:1, :], vl[1:2, :]], axis=1).astype(F32)
    level = jnp.broadcast_to(level, (2 * BLOCK, 2 * BLOCK)).T
    index = lax.broadcasted_iota(jnp.int32, (1, entries), 1).astype(F32)
    angles = level * jnp.exp(-math.log(10000.0) * index / entries)
    embed = jnp.concatenate([jnp.cos(angles), jnp.sin(angles)], axis=1).astype(BF16)
    loads[3].wait()
    mod[...] = jnp.dot(embed, vm[...], preferred_element_type=F32)

    def tell(batch, p):
        return remote(
            meta.at[batch, p // 3], meta.at[batch, p], m_send.at[batch, p - 1], m_recv.at[batch, p - 1],
            along(batch, OFFSET[p % 3 + p // 3], 0, 0),
        )

    for batch in range(2):
        for p in (1, 2):
            tell(batch, p).start()

    def spread(batch, part, way):
        rows = pl.ds(part * PIECE, PIECE)
        return remote(
            gathered.at[batch, 0, rows], gathered.at[batch, 1 + way, rows],
            g_send.at[batch, way, part], g_recv.at[batch, way, part], along(batch, 1 - 2 * way, 0, 0),
        )

    def normalize(batch, part):
        rows = pl.ds(part * PIECE, PIECE)
        got(arrived.at[batch, rows], z_recv.at[batch + 2 * part])
        values = arrived[batch, rows, :].astype(F32)
        mean_square = jnp.mean(values * values, axis=1, keepdims=True)
        own = pl.ds(batch * BLOCK + part * PIECE, PIECE)
        normed = values * lax.rsqrt(mean_square + epsilon) * (1.0 + mod[own, :features]) + mod[own, features:]
        gathered[batch, 0, rows, :] = normed.astype(BF16)
        spread(batch, part, 0).start()
        spread(batch, part, 1).start()

    def spread_in(batch, way, half):
        for part in (2 * half, 2 * half + 1):
            got(gathered.at[batch, 1 + way, pl.ds(part * PIECE, PIECE)], g_recv.at[batch, way, part])

    def hand_on(batch, way):
        rows = pl.ds(way * HALF, HALF)
        return remote(
            gathered.at[batch, 1 + way, rows], gathered.at[batch, 3, rows],
            gf_send.at[batch, way], gf_recv.at[batch, way], along(batch, 1 - 2 * way, 0, 0),
        )

    def forward(batch, way):
        spread_in(batch, way, way)
        hand_on(batch, way).start()
        if way == 0:
            got(meta.at[batch, 1], m_recv.at[batch, 0])
            tell(batch, 3).start()

    pick = lax.broadcasted_iota(jnp.int32, (PICKS, 2 * BLOCK), 0)
    far, other_seat, slot_of = pick // (2 * SLOTS), (pick // SLOTS) % 2, pick % SLOTS
    seat_of = core + other_seat * (1 - 2 * core)
    wanted = []
    for batch in range(2):
        if batch == 0:
            line = x * 8 + ((y + far) % SIDE) * 2
        else:
            line = ((x + far) % SIDE) * 8 + y * 2
        wanted.append(((line + seat_of) * SLOTS + slot_of).astype(F32))

    def exchange(p, batch, block):
        step, other = block // 2, block % 2
        if step == 2:
            return remote(
                picked.at[p, batch, block], passed.at[p, batch, other], b_send.at[p, batch], f_recv.at[p, batch],
                along(batch, 0, 1 - 2 * other, 0),
            )
        return remote(
            picked.at[p, batch, block], rows_in.at[p, batch, block], b_send.at[p, batch], b_recv.at[p, batch],
            along(batch, 0, step, other),
        )

    order = (4, 5, 2, 6, 3, 7, 1)

    def select(batch, p):
        if p == 3:
            for way in range(2):
                got(gathered.at[batch, 3, pl.ds(way * HALF, HALF)], gf_recv.at[batch, way])
        elif p:
            spread_in(batch, p - 1, 2 - p)
        if p > 1:
            got(meta.at[batch, p], m_recv.at[batch, p - 1])
        hit = jnp.zeros((PICKS, 2 * BLOCK), F32)
        worth = jnp.zeros((PICKS, 2 * BLOCK), F32)
        for k in range(top):
            same = meta[batch, p, k : k + 1, :] == wanted[batch]
            hit = jnp.where(same, 1.0, hit)
            worth = jnp.where(same, meta[batch, p, 8 + k : 9 + k, :], worth)
        chosen = jnp.dot(hit[:, :BLOCK].astype(BF16), gathered[batch, p], preferred_element_type=F32)
        chosen = chosen.astype(BF16).reshape(2 * SIDE, SLOTS, features)
        picked[p, batch] = chosen
        rows_in[p, batch, 0] = chosen[0]
        for block in order:
            exchange(p, batch, block).start()
        worth = worth.T
        high = worth[:BLOCK].astype(BF16)
        weigh[batch, p, :BLOCK, :] = high
        weigh[batch, p, BLOCK:, :] = (worth[:BLOCK] - high.astype(F32)).astype(BF16)

    def pass_on(p, batch):
        return [
            remote(
                passed.at[p, batch, other], rows_in.at[p, batch, 4 + other], f_send.at[p, batch], b_recv.at[p, batch],
                along(batch, 0, 1 - 2 * other, other),
            )
            for other in range(2)
        ]

    def move_on(p, batch):
        got(passed.at[p, batch], f_recv.at[p, batch])
        for copy in pass_on(p, batch):
            copy.start()

    for part in (0, 1):
        for batch in range(2):
            normalize(batch, part)
    normalize(0, 2)
    forward(0, 0)
    normalize(1, 2)
    forward(1, 0)
    normalize(0, 3)
    normalize(1, 3)
    select(0, 0)
    select(1, 0)
    forward(0, 1)
    forward(1, 1)
    move_on(0, 0)
    move_on(0, 1)
    select(0, 1)
    select(1, 1)
    select(0, 2)
    select(1, 2)
    move_on(1, 0)
    move_on(1, 1)
    select(0, 3)
    select(1, 3)

    for load in loads[4:]:
        load.wait()

    def back(p, batch, block):
        step, other = block // 2, block % 2
        if step == 2:
            return remote(
                rows_out.at[p, batch, block], passed_back.at[p, batch, other], o_send.at[p, batch],
                p_recv.at[p, batch], along(batch, 0, 2 * other - 1, 0),
            )
        return remote(
            rows_out.at[p, batch, block], returned.at[p, batch, block], o_send.at[p, batch], o_recv.at[p, batch],
            along(batch, 0, 4 - step, other),
        )

    def pass_back(p, batch):
        return [
            remote(
                passed_back.at[p, batch, other], returned.at[p, batch, 4 + other], p_send.at[p, batch],
                o_recv.at[p, batch], along(batch, 0, 2 * other - 1, other),
            )
            for other in range(2)
        ]

    def move_back(p):
        for batch in range(2):
            got(passed_back.at[p, batch], p_recv.at[p, batch])
            for copy in pass_back(p, batch):
                copy.start()

    def send_back(p):
        for block in order:
            for batch in range(2):
                back(p, batch, block).start()

    def work(p, carry):
        @pl.when(p == 1)
        def _():
            move_on(2, 0)
            move_on(2, 1)
            move_on(3, 0)
            move_on(3, 1)

        for batch in range(2):
            got(rows_in.at[p, batch, pl.ds(1, 7)], b_recv.at[p, batch])
        rows = rows_in[p].reshape(2 * PICKS, features)
        gate_part = jnp.dot(rows, vg[...], preferred_element_type=F32)
        up_part = jnp.dot(rows, vu[...], preferred_element_type=F32)
        hidden = (gate_part / (1.0 + jnp.exp(-gate_part)) * up_part).astype(BF16)
        produced = jnp.dot(hidden, vd[...], preferred_element_type=F32).astype(BF16)
        produced = produced.reshape(2, 2 * SIDE, SLOTS, features)
        rows_out[p] = produced
        for batch in range(2):
            returned[p, batch, 0] = produced[batch, 0]

        @pl.when(p > 1)
        def _():
            move_back(p - 1)

        @pl.when(p > 0)
        def _():
            send_back(p)

        return carry

    lax.fori_loop(0, SIDE, work, 0)

    def add_up(p, batch):
        got(returned.at[p, batch, pl.ds(1, 7)], o_recv.at[p, batch])
        rows = returned[p, batch].reshape(PICKS, features)
        both = jnp.dot(weigh[batch, p], rows, preferred_element_type=F32)
        return both[:BLOCK] + both[BLOCK:]

    def sum_half(batch, way, piece):
        return remote(
            far_part.at[batch, way, piece], half_in.at[batch, way, piece], h_send.at[batch, way, piece],
            h_recv.at[batch, way, piece], along(batch, 2 * way - 1, 0, 0),
        )

    def sum_home(batch, way, part):
        return remote(
            near_part.at[batch, way, part], part_in.at[batch, way, part], q_send.at[batch, way, part],
            q_recv.at[batch, way, part], along(batch, 2 * way - 1, 0, 0),
        )

    def add_own(batch, carry):
        total[batch] = add_up(0, batch) + arrived[batch].astype(F32)
        return carry

    def add_near(way):
        def add(batch, carry):
            near = add_up(1 + way, batch).reshape(4, PIECE, features)
            for piece in range(2):
                part = 2 * (1 - way) + piece
                near_held[batch, way, piece] = near[2 * way + piece]
                near_part[batch, way, part] = near[part].astype(BF16)
                sum_home(batch, way, part).start()
            return carry

        return add

    def add_far(batch, carry):
        far_part[batch] = add_up(3, batch).astype(BF16).reshape(2, 2, PIECE, features)
        for piece in range(2):
            for way in range(2):
                sum_half(batch, way, piece).start()
        return carry

    lax.fori_loop(0, 2, add_near(0), 0)
    move_back(3)
    send_back(0)
    lax.fori_loop(0, 2, add_near(1), 0)
    lax.fori_loop(0, 2, add_far, 0)
    move_back(0)

    def add_half(piece, carry):
        for batch in range(2):
            for way in range(2):
                got(half_in.at[batch, way, piece], h_recv.at[batch, way, piece])
                part = 2 * way + piece
                held = near_held[batch, way, piece] + half_in[batch, way, piece].astype(F32)
                near_part[batch, way, part] = held.astype(BF16)
                sum_home(batch, way, part).start()
        return carry

    lax.fori_loop(0, 2, add_half, 0)
    lax.fori_loop(0, 2, add_own, 0)

    def finish(piece, carry):
        for batch in range(2):
            for half in range(2):
                part = 2 * half + piece
                for way in range(2):
                    got(part_in.at[batch, way, part], q_recv.at[batch, way, part])
                rows = pl.ds(pl.multiple_of(part * PIECE, PIECE), PIECE)
                sums = part_in[batch, 0, part].astype(F32) + part_in[batch, 1, part].astype(F32)
                out[batch, rows, :] = (total[batch, rows, :] + sums).astype(BF16)
        return carry

    lax.fori_loop(0, 2, finish, 0)

    for piece in range(8):
        shift(piece).wait_send()
    for batch in range(2):
        for p in (1, 2, 3):
            tell(batch, p).wait_send()
        for way in range(2):
            for part in range(4):
                spread(batch, part, way).wait_send()
            hand_on(batch, way).wait_send()
            for piece in range(2):
                sum_half(batch, way, piece).wait_send()
            for part in range(4):
                sum_home(batch, way, part).wait_send()
        for p in range(SIDE):
            left(picked.at[p, batch, pl.ds(1, 7)], b_send.at[p, batch])
            left(passed.at[p, batch], f_send.at[p, batch])
            left(rows_out.at[p, batch, pl.ds(1, 7)], o_send.at[p, batch])
            left(passed_back.at[p, batch], p_send.at[p, batch])


def shards(emitted, levels, expert_ids, gate_values, w_gate, w_up, w_down, w_mod):
    batches, rows, features = emitted.shape[1:]
    top, inner = expert_ids.shape[3], w_gate.shape[3]
    tokens = batches * rows
    ids = expert_ids.transpose(0, 3, 1, 2)
    gates = gate_values.transpose(0, 3, 1, 2)
    anywhere, vmem = pl.BlockSpec(memory_space=pl.ANY), pl.BlockSpec(memory_space=pltpu.VMEM)
    dma = pltpu.SemaphoreType.DMA
    lines = pltpu.VMEM((SIDE, 2, 2 * SIDE, SLOTS, features), BF16)
    held = [
        pltpu.with_memory_space_constraint(array, pltpu.HBM)
        for array in (emitted, levels, ids, gates, w_gate, w_up, w_down, w_mod)
    ]
    out = pl.pallas_call(
        functools.partial(layer_kernel, lax.axis_size("section"), top),
        out_shape=jax.ShapeDtypeStruct((batches, rows, features), BF16),
        in_specs=[anywhere] * 8,
        out_specs=vmem,
        scratch_shapes=[
            pltpu.VMEM((features, inner), BF16),
            pltpu.VMEM((features, inner), BF16),
            pltpu.VMEM((inner, features), BF16),
            pltpu.VMEM(w_mod.shape[1:], BF16),
            pltpu.VMEM((batches, rows), jnp.int32),
            pltpu.VMEM((top, batches, rows), jnp.int32),
            pltpu.VMEM((top, batches, rows), F32),
            pltpu.VMEM((tokens, 2 * features), F32),
            pltpu.VMEM((2, SIDE, 16, 2 * BLOCK), F32),
            pltpu.VMEM((2, SIDE, 2 * BLOCK, PICKS), BF16),
            pltpu.VMEM((2, BLOCK, features), BF16),
            pltpu.VMEM((2, SIDE, BLOCK, features), BF16),
            lines,
            pltpu.VMEM((SIDE, 2, 2, SLOTS, features), BF16),
            lines,
            lines,
            pltpu.VMEM((SIDE, 2, 2, SLOTS, features), BF16),
            lines,
            pltpu.VMEM((2, 2, 2, PIECE, features), BF16),
            pltpu.VMEM((2, 2, 4, PIECE, features), BF16),
            pltpu.VMEM((2, 2, 2, PIECE, features), F32),
            pltpu.VMEM((2, 2, 2, PIECE, features), BF16),
            pltpu.VMEM((2, 2, 4, PIECE, features), BF16),
            pltpu.VMEM((2, BLOCK, features), F32),
            dma((7,)), dma((8,)), dma((8,)),
            dma((2, 3)), dma((2, 3)),
            dma((2, 2, 4)), dma((2, 2, 4)), dma((2, 2)), dma((2, 2)),
            dma((SIDE, 2)), dma((SIDE, 2)), dma((SIDE, 2)), dma((SIDE, 2)),
            dma((SIDE, 2)), dma((SIDE, 2)), dma((SIDE, 2)), dma((SIDE, 2)),
            dma((2, 2, 2)), dma((2, 2, 2)), dma((2, 2, 4)), dma((2, 2, 4)),
        ],
        compiler_params=pltpu.CompilerParams(
            collective_id=0, has_side_effects=True, vmem_limit_bytes=52 * 1024 * 1024
        ),
    )(*held)
    return out[None]


def solution(mesh):
    placed = (
        P("section", None, "expert", None),
        P("section", None, "expert"),
        P("section", None, "expert", None),
        P("section", None, "expert", None),
        P("section", "expert", None, None),
        P("section", "expert", None, None),
        P("section", "expert", None, None),
        P("section", None, None),
    )
    return jax.shard_map(
        shards,
        mesh=mesh,
        in_specs=placed,
        out_specs=P("section", None, "expert", None),
        check_vma=False,
    )
```

```python
import functools
import math

import jax
import jax.numpy as jnp
from jax import lax
from jax.experimental import pallas as pl
from jax.experimental.pallas import tpu as pltpu
from jax.sharding import PartitionSpec as P

epsilon = 1e-06
MESH = pl.DeviceIdType.MESH
F32, BF16 = jnp.float32, jnp.bfloat16
SIDE = 4
SLOTS = 16
BLOCK = 64
HALF = BLOCK // 2
PIECE = BLOCK // 4
OFFSET = (0, 1, 3, 2)
PICKS = SIDE * 2 * SLOTS


def layer_kernel(
    sections, top,
    emitted, levels, ids, gates, w_gate, w_up, w_down, w_mod,
    out,
    vg, vu, vd, vm, vl, vi, vw, mod, meta, weigh,
    arrived, gathered, picked, passed, rows_in, rows_out, passed_back, returned,
    far_part, near_part, near_held, half_in, part_in, total,
    load_sem, z_send, z_recv, m_send, m_recv, g_send, g_recv, gf_send, gf_recv,
    b_send, b_recv, f_recv, f_send, o_send, o_recv, p_recv, p_send, h_send, h_recv, q_send, q_recv,
):
    section = lax.axis_index("section")
    place = lax.axis_index("expert")
    x, y, core = place // 8, (place // 2) % SIDE, place % 2
    features = arrived.shape[2]

    def at(dx, dy, other):
        seat = core + other * (1 - 2 * core)
        return (section, ((x + dx + 8) % SIDE) * 8 + ((y + dy + 8) % SIDE) * 2 + seat)

    def along(batch, da, db, other):
        return at(da + batch * (db - da), db + batch * (da - db), other)

    def remote(src, dst, send, recv, device):
        return pltpu.make_async_remote_copy(
            src_ref=src, dst_ref=dst, send_sem=send, recv_sem=recv, device_id=device, device_id_type=MESH
        )

    def got(dst, recv):
        remote(dst, dst, recv, recv, (section, place)).wait_recv()

    def left(src, send):
        remote(src, src, send, send, (section, place)).wait_send()

    after = ((section + 1) % sections, place)
    ahead = ((section + sections - 1) % sections, place)

    barrier = pltpu.get_barrier_semaphore()
    friends = [after, ahead, at(0, 0, 1), at(2, 0, 0), at(0, 2, 0)]
    for step in (1, -1):
        for other in (0, 1):
            friends += [at(step, 0, other), at(0, step, other)]
    for friend in friends:
        pl.semaphore_signal(barrier, inc=1, device_id=friend, device_id_type=MESH)

    sources = (levels.at[0], ids.at[0], gates.at[0], w_mod.at[0], w_gate.at[0, 0], w_up.at[0, 0], w_down.at[0, 0])
    targets = (vl, vi, vw, vm, vg, vu, vd)
    loads = [pltpu.make_async_copy(a, b, load_sem.at[i]) for i, (a, b) in enumerate(zip(sources, targets))]
    for load in loads[:4]:
        load.start()
    pl.semaphore_wait(barrier, len(friends))

    def shift(piece):
        batch, rows = piece % 2, pl.ds((piece // 2) * PIECE, PIECE)
        return remote(
            emitted.at[0, batch, rows], arrived.at[batch, rows], z_send.at[piece], z_recv.at[piece], after
        )

    for piece in range(8):
        shift(piece).start()
    for load in loads[4:]:
        load.start()

    for load in loads[:3]:
        load.wait()

    experts = SIDE * SIDE * 2
    name = lax.broadcasted_iota(jnp.int32, (experts, BLOCK), 0)
    row = lax.broadcasted_iota(jnp.int32, (BLOCK, BLOCK), 0)
    col = lax.broadcasted_iota(jnp.int32, (BLOCK, BLOCK), 1)
    earlier = jnp.where(row < col, 1.0, 0.0).astype(BF16)
    for batch in range(2):
        meta[batch, 0] = jnp.full((16, 2 * BLOCK), -1.0, F32)
        numbers = [vi[k, batch : batch + 1, :] for k in range(top)]
        named = jnp.zeros((experts, BLOCK), F32)
        for number in numbers:
            named = named + jnp.where(number == name, 1.0, 0.0)
        before = jnp.dot(named.astype(BF16), earlier, preferred_element_type=F32)
        for k, number in enumerate(numbers):
            slot = jnp.sum(jnp.where(number == name, before, 0.0), axis=0, keepdims=True)
            meta[batch, 0, k : k + 1, :BLOCK] = number.astype(F32) * SLOTS + slot
            meta[batch, 0, 8 + k : 9 + k, :BLOCK] = vw[k, batch : batch + 1, :]

    entries = w_mod.shape[1] // 2
    level = jnp.concatenate([vl[0:1, :], vl[1:2, :]], axis=1).astype(F32)
    level = jnp.broadcast_to(level, (2 * BLOCK, 2 * BLOCK)).T
    index = lax.broadcasted_iota(jnp.int32, (1, entries), 1).astype(F32)
    angles = level * jnp.exp(-math.log(10000.0) * index / entries)
    embed = jnp.concatenate([jnp.cos(angles), jnp.sin(angles)], axis=1).astype(BF16)
    loads[3].wait()
    mod[...] = jnp.dot(embed, vm[...], preferred_element_type=F32)

    def tell(batch, p):
        return remote(
            meta.at[batch, 0], meta.at[batch, p], m_send.at[batch, p - 1], m_recv.at[batch, p - 1],
            along(batch, OFFSET[p], 0, 0),
        )

    for batch in range(2):
        for p in (1, 2, 3):
            tell(batch, p).start()

    def spread(batch, part, way):
        rows = pl.ds(part * PIECE, PIECE)
        return remote(
            gathered.at[batch, 0, rows], gathered.at[batch, 1 + way, rows],
            g_send.at[batch, way, part], g_recv.at[batch, way, part], along(batch, 1 - 2 * way, 0, 0),
        )

    def normalize(batch, part):
        rows = pl.ds(part * PIECE, PIECE)
        got(arrived.at[batch, rows], z_recv.at[batch + 2 * part])
        values = arrived[batch, rows, :].astype(F32)
        mean_square = jnp.mean(values * values, axis=1, keepdims=True)
        own = pl.ds(batch * BLOCK + part * PIECE, PIECE)
        normed = values * lax.rsqrt(mean_square + epsilon) * (1.0 + mod[own, :features]) + mod[own, features:]
        gathered[batch, 0, rows, :] = normed.astype(BF16)
        spread(batch, part, 0).start()
        spread(batch, part, 1).start()

    def spread_in(batch, way, half):
        for part in (2 * half, 2 * half + 1):
            got(gathered.at[batch, 1 + way, pl.ds(part * PIECE, PIECE)], g_recv.at[batch, way, part])

    def hand_on(batch, way):
        rows = pl.ds(way * HALF, HALF)
        return remote(
            gathered.at[batch, 1 + way, rows], gathered.at[batch, 3, rows],
            gf_send.at[batch, way], gf_recv.at[batch, way], along(batch, 1 - 2 * way, 0, 0),
        )

    def forward(batch, way):
        spread_in(batch, way, way)
        hand_on(batch, way).start()

    pick = lax.broadcasted_iota(jnp.int32, (PICKS, 2 * BLOCK), 0)
    far, other_seat, slot_of = pick // (2 * SLOTS), (pick // SLOTS) % 2, pick % SLOTS
    seat_of = core + other_seat * (1 - 2 * core)
    wanted = []
    for batch in range(2):
        if batch == 0:
            line = x * 8 + ((y + far) % SIDE) * 2
        else:
            line = ((x + far) % SIDE) * 8 + y * 2
        wanted.append(((line + seat_of) * SLOTS + slot_of).astype(F32))

    def exchange(p, batch, block):
        step, other = block // 2, block % 2
        if step == 2:
            return remote(
                picked.at[p, batch, block], passed.at[p, batch, other], b_send.at[p, batch], f_recv.at[p, batch],
                along(batch, 0, 1 - 2 * other, 0),
            )
        return remote(
            picked.at[p, batch, block], rows_in.at[p, batch, block], b_send.at[p, batch], b_recv.at[p, batch],
            along(batch, 0, step, other),
        )

    order = (4, 5, 2, 6, 3, 7, 1)

    def select(batch, p):
        if p == 3:
            for way in range(2):
                got(gathered.at[batch, 3, pl.ds(way * HALF, HALF)], gf_recv.at[batch, way])
        elif p:
            spread_in(batch, p - 1, 2 - p)
        if p:
            got(meta.at[batch, p], m_recv.at[batch, p - 1])
        hit = jnp.zeros((PICKS, 2 * BLOCK), F32)
        worth = jnp.zeros((PICKS, 2 * BLOCK), F32)
        for k in range(top):
            same = meta[batch, p, k : k + 1, :] == wanted[batch]
            hit = jnp.where(same, 1.0, hit)
            worth = jnp.where(same, meta[batch, p, 8 + k : 9 + k, :], worth)
        chosen = jnp.dot(hit[:, :BLOCK].astype(BF16), gathered[batch, p], preferred_element_type=F32)
        chosen = chosen.astype(BF16).reshape(2 * SIDE, SLOTS, features)
        picked[p, batch] = chosen
        rows_in[p, batch, 0] = chosen[0]
        for block in order:
            exchange(p, batch, block).start()
        worth = worth.T
        high = worth[:BLOCK].astype(BF16)
        weigh[batch, p, :BLOCK, :] = high
        weigh[batch, p, BLOCK:, :] = (worth[:BLOCK] - high.astype(F32)).astype(BF16)

    def pass_on(p, batch):
        return [
            remote(
                passed.at[p, batch, other], rows_in.at[p, batch, 4 + other], f_send.at[p, batch], b_recv.at[p, batch],
                along(batch, 0, 1 - 2 * other, other),
            )
            for other in range(2)
        ]

    def move_on(p, batch):
        got(passed.at[p, batch], f_recv.at[p, batch])
        for copy in pass_on(p, batch):
            copy.start()

    for part in (0, 1):
        for batch in range(2):
            normalize(batch, part)
    normalize(0, 2)
    forward(0, 0)
    normalize(1, 2)
    forward(1, 0)
    normalize(0, 3)
    normalize(1, 3)
    select(0, 0)
    select(1, 0)
    forward(0, 1)
    forward(1, 1)
    move_on(0, 0)
    move_on(0, 1)
    select(0, 1)
    select(1, 1)
    select(0, 2)
    select(1, 2)
    move_on(1, 0)
    move_on(1, 1)
    select(0, 3)
    select(1, 3)

    for load in loads[4:]:
        load.wait()

    def back(p, batch, block):
        step, other = block // 2, block % 2
        if step == 2:
            return remote(
                rows_out.at[p, batch, block], passed_back.at[p, batch, other], o_send.at[p, batch],
                p_recv.at[p, batch], along(batch, 0, 2 * other - 1, 0),
            )
        return remote(
            rows_out.at[p, batch, block], returned.at[p, batch, block], o_send.at[p, batch], o_recv.at[p, batch],
            along(batch, 0, 4 - step, other),
        )

    def pass_back(p, batch):
        return [
            remote(
                passed_back.at[p, batch, other], returned.at[p, batch, 4 + other], p_send.at[p, batch],
                o_recv.at[p, batch], along(batch, 0, 2 * other - 1, other),
            )
            for other in range(2)
        ]

    def move_back(p):
        for batch in range(2):
            got(passed_back.at[p, batch], p_recv.at[p, batch])
            for copy in pass_back(p, batch):
                copy.start()

    def send_back(p):
        for block in order:
            for batch in range(2):
                back(p, batch, block).start()

    def work(p, carry):
        @pl.when(p == 1)
        def _():
            move_on(2, 0)
            move_on(2, 1)
            move_on(3, 0)
            move_on(3, 1)

        for batch in range(2):
            got(rows_in.at[p, batch, pl.ds(1, 7)], b_recv.at[p, batch])
        rows = rows_in[p].reshape(2 * PICKS, features)
        gate_part = jnp.dot(rows, vg[...], preferred_element_type=F32)
        up_part = jnp.dot(rows, vu[...], preferred_element_type=F32)
        hidden = (gate_part / (1.0 + jnp.exp(-gate_part)) * up_part).astype(BF16)
        produced = jnp.dot(hidden, vd[...], preferred_element_type=F32).astype(BF16)
        produced = produced.reshape(2, 2 * SIDE, SLOTS, features)
        rows_out[p] = produced
        for batch in range(2):
            returned[p, batch, 0] = produced[batch, 0]

        @pl.when(p > 1)
        def _():
            move_back(p - 1)

        @pl.when(p > 0)
        def _():
            send_back(p)

        return carry

    lax.fori_loop(0, SIDE, work, 0)

    def add_up(p, batch):
        got(returned.at[p, batch, pl.ds(1, 7)], o_recv.at[p, batch])
        rows = returned[p, batch].reshape(PICKS, features)
        both = jnp.dot(weigh[batch, p], rows, preferred_element_type=F32)
        return both[:BLOCK] + both[BLOCK:]

    def sum_half(batch, way):
        return remote(
            far_part.at[batch, way], half_in.at[batch, way], h_send.at[batch, way], h_recv.at[batch, way],
            along(batch, 2 * way - 1, 0, 0),
        )

    def sum_home(batch, way, part):
        return remote(
            near_part.at[batch, way, part], part_in.at[batch, way, part], q_send.at[batch, way, part],
            q_recv.at[batch, way, part], along(batch, 2 * way - 1, 0, 0),
        )

    def add_own(batch, carry):
        total[batch] = add_up(0, batch) + arrived[batch].astype(F32)
        return carry

    def add_near(way):
        def add(batch, carry):
            near = add_up(1 + way, batch).reshape(2, HALF, features)
            near_held[batch, way] = near[way]
            near_part[batch, way, 1 - way] = near[1 - way].astype(BF16)
            sum_home(batch, way, 1 - way).start()
            return carry

        return add

    def add_far(batch, carry):
        far_part[batch] = add_up(3, batch).astype(BF16).reshape(2, HALF, features)
        sum_half(batch, 0).start()
        sum_half(batch, 1).start()
        return carry

    lax.fori_loop(0, 2, add_near(0), 0)
    move_back(3)
    send_back(0)
    lax.fori_loop(0, 2, add_near(1), 0)
    lax.fori_loop(0, 2, add_far, 0)
    move_back(0)

    def add_half(batch, carry):
        for way in range(2):
            got(half_in.at[batch, way], h_recv.at[batch, way])
            near_part[batch, way, way] = (near_held[batch, way] + half_in[batch, way].astype(F32)).astype(BF16)
            sum_home(batch, way, way).start()
        return carry

    lax.fori_loop(0, 2, add_half, 0)
    lax.fori_loop(0, 2, add_own, 0)

    def finish(batch, carry):
        for part in range(2):
            for way in range(2):
                got(part_in.at[batch, way, part], q_recv.at[batch, way, part])
            rows = pl.ds(part * HALF, HALF)
            sums = part_in[batch, 0, part].astype(F32) + part_in[batch, 1, part].astype(F32)
            out[batch, rows, :] = (total[batch, rows, :] + sums).astype(BF16)
        return carry

    lax.fori_loop(0, 2, finish, 0)

    for piece in range(8):
        shift(piece).wait_send()
    for batch in range(2):
        for p in (1, 2, 3):
            tell(batch, p).wait_send()
        for way in range(2):
            for part in range(4):
                spread(batch, part, way).wait_send()
            hand_on(batch, way).wait_send()
            sum_half(batch, way).wait_send()
            sum_home(batch, way, 0).wait_send()
            sum_home(batch, way, 1).wait_send()
        for p in range(SIDE):
            left(picked.at[p, batch, pl.ds(1, 7)], b_send.at[p, batch])
            left(passed.at[p, batch], f_send.at[p, batch])
            left(rows_out.at[p, batch, pl.ds(1, 7)], o_send.at[p, batch])
            left(passed_back.at[p, batch], p_send.at[p, batch])


def shards(emitted, levels, expert_ids, gate_values, w_gate, w_up, w_down, w_mod):
    batches, rows, features = emitted.shape[1:]
    top, inner = expert_ids.shape[3], w_gate.shape[3]
    tokens = batches * rows
    ids = expert_ids.transpose(0, 3, 1, 2)
    gates = gate_values.transpose(0, 3, 1, 2)
    anywhere, vmem = pl.BlockSpec(memory_space=pl.ANY), pl.BlockSpec(memory_space=pltpu.VMEM)
    dma = pltpu.SemaphoreType.DMA
    lines = pltpu.VMEM((SIDE, 2, 2 * SIDE, SLOTS, features), BF16)
    held = [
        pltpu.with_memory_space_constraint(array, pltpu.HBM)
        for array in (emitted, levels, ids, gates, w_gate, w_up, w_down, w_mod)
    ]
    out = pl.pallas_call(
        functools.partial(layer_kernel, lax.axis_size("section"), top),
        out_shape=jax.ShapeDtypeStruct((batches, rows, features), BF16),
        in_specs=[anywhere] * 8,
        out_specs=vmem,
        scratch_shapes=[
            pltpu.VMEM((features, inner), BF16),
            pltpu.VMEM((features, inner), BF16),
            pltpu.VMEM((inner, features), BF16),
            pltpu.VMEM(w_mod.shape[1:], BF16),
            pltpu.VMEM((batches, rows), jnp.int32),
            pltpu.VMEM((top, batches, rows), jnp.int32),
            pltpu.VMEM((top, batches, rows), F32),
            pltpu.VMEM((tokens, 2 * features), F32),
            pltpu.VMEM((2, SIDE, 16, 2 * BLOCK), F32),
            pltpu.VMEM((2, SIDE, 2 * BLOCK, PICKS), BF16),
            pltpu.VMEM((2, BLOCK, features), BF16),
            pltpu.VMEM((2, SIDE, BLOCK, features), BF16),
            lines,
            pltpu.VMEM((SIDE, 2, 2, SLOTS, features), BF16),
            lines,
            lines,
            pltpu.VMEM((SIDE, 2, 2, SLOTS, features), BF16),
            lines,
            pltpu.VMEM((2, 2, HALF, features), BF16),
            pltpu.VMEM((2, 2, 2, HALF, features), BF16),
            pltpu.VMEM((2, 2, HALF, features), F32),
            pltpu.VMEM((2, 2, HALF, features), BF16),
            pltpu.VMEM((2, 2, 2, HALF, features), BF16),
            pltpu.VMEM((2, BLOCK, features), F32),
            dma((7,)), dma((8,)), dma((8,)),
            dma((2, 3)), dma((2, 3)),
            dma((2, 2, 4)), dma((2, 2, 4)), dma((2, 2)), dma((2, 2)),
            dma((SIDE, 2)), dma((SIDE, 2)), dma((SIDE, 2)), dma((SIDE, 2)),
            dma((SIDE, 2)), dma((SIDE, 2)), dma((SIDE, 2)), dma((SIDE, 2)),
            dma((2, 2)), dma((2, 2)), dma((2, 2, 2)), dma((2, 2, 2)),
        ],
        compiler_params=pltpu.CompilerParams(
            collective_id=0, has_side_effects=True, vmem_limit_bytes=52 * 1024 * 1024
        ),
    )(*held)
    return out[None]


def solution(mesh):
    placed = (
        P("section", None, "expert", None),
        P("section", None, "expert"),
        P("section", None, "expert", None),
        P("section", None, "expert", None),
        P("section", "expert", None, None),
        P("section", "expert", None, None),
        P("section", "expert", None, None),
        P("section", None, None),
    )
    return jax.shard_map(
        shards,
        mesh=mesh,
        in_specs=placed,
        out_specs=P("section", None, "expert", None),
        check_vma=False,
    )
```
